256 devices in a mesh: tok: 32 (over x, z_lo, core), exp: 8 (over z_hi, y).
Axes of the slice: x: 4, y: 4, z: 8 (z_hi: 2, z_lo: 4; z = z_hi * 4 + z_lo), core: 2. Of those that a mesh axis runs over, the one named last changes fastest.
Arguments:
- tokens: bfloat16 [24576, 4096], P('tok'), may hold values from -6 to 6
- route_ids: int32 [24576, 8], P('tok'), may hold values from 0 to 127, all different within a row; in each aligned block of 768 rows (0 to 767, 768 to 1535, ...) at most 128 rows name the same one
- whiten: bfloat16 [16, 4096, 4096], P('exp', 'tok'), may hold values from -0.09375 to 0.09375
- deltas: bfloat16 [16, 4096, 1536], P('exp', 'tok'), may hold values from -6 to 6
- basis: bfloat16 [4096, 768], P('exp'), may hold values from -0.09375 to 0.09375
Outputs:
- gram: float32 [4096, 1, 4096], P('tok', None, 'exp')
- coefficients: float32 [768, 16, 1536], P('tok', 'exp')
- basis_gram: float32 [768, 768], P('tok')
The draws below stay inside these ranges and needn't reach their ends.
Inputs may be any that keep to these rules, and one draw needn't show every extreme that they name: `route_ids`: each row names 8 different experts; among the rows of one device (aligned blocks of 768 rows) no expert is named by more than 128 rows.
All inputs are finite; a program needn't handle non-finite values.
Results may differ from the reference program's by a relative error of at most 0.0029.
Values may be sent and summed in bfloat16 or wider, within the bound.
A program may use at most 128 MiB of HBM per device.

```python
import math
import jax
import jax.numpy as jnp
import numpy as np
from jax import lax

D = 4096
H = 1536
NROUTE = 128
TOP = 8
R = 768
GRAM_EXP = 1
CAP = 128
TOK_DEV = 768
TOKENS = 24576
EXPERTS = 16


def steps_of(key, shape, pieces, least, largest):
    gain, own = 1.0, jax.random.fold_in(key, 6)
    for axis_at, parts in pieces:
        heights = jnp.exp(jax.random.uniform(jax.random.fold_in(own, axis_at), (parts,), jnp.float32, least / len(pieces), largest / len(pieces)))
        gain = gain * jnp.repeat(heights, shape[axis_at] // parts).reshape([-1 if axis == axis_at else 1 for axis in range(len(shape))])
    return gain


def deal_out(rng, own, number, rows, count, top, most, skew):
    ranking = jax.random.permutation(rng, count)
    heavy_load, common = portions_of(count, rows * top, most, skew, True), portions_of(count, rows * top, most, skew, False)
    places = jnp.arange(count)

    def named(lengths, offset_by):
        used = int((lengths > 0).sum())
        fixed = max(1, used // 4)
        moved = fixed + (places - fixed + offset_by * (used - fixed)) % max(1, count - fixed)
        return jnp.zeros((count,), jnp.int32).at[ranking[jnp.where(places < fixed, places, moved)]].set(jnp.asarray(lengths, jnp.int32))

    lengths = jnp.where(number % 4 == 0, named(heavy_load, number // 4), named(common, number - number // 4 - 1))
    mixed = jax.random.permutation(jax.random.fold_in(own, 3), count)
    donor, taker = mixed[0:count // 2 * 2:2], mixed[1:count // 2 * 2:2]
    room = jnp.minimum(lengths[donor] - 1, most - lengths[taker]) // 2
    room = jnp.where((donor == ranking[0]) | (taker == ranking[0]) | (lengths[taker] == 0), 0, jnp.maximum(room, 0))
    moved = jax.random.randint(jax.random.fold_in(own, 4), (count // 2,), 0, 1 << 20) % (room + 1)
    lengths = lengths.at[donor].add(-moved).at[taker].add(moved)
    items = jnp.searchsorted(jnp.cumsum(lengths), jnp.arange(rows * top), side="right").astype(jnp.int32)
    grid = items.reshape(top, rows).T
    grid = grid[jax.random.permutation(jax.random.fold_in(own, 1), rows)]
    offset_by = jax.random.randint(jax.random.fold_in(own, 2), (rows, 1), 0, top)
    return jnp.take_along_axis(grid, (jnp.arange(top)[None, :] + offset_by) % top, axis=1)


def portions_of(number_of, total, bound, slope, full):
    portions = [(1 << 20) // math.isqrt(rank ** slope) + 1 for rank in range(1, number_of + 1)]
    largest = bound if full else min(bound, max(-(-total // number_of), total * portions[0] // sum(portions)))
    least = 1 if total - largest >= number_of - 1 else 0
    counts, surplus = [largest] + [least] * (number_of - 1), total - largest - least * (number_of - 1)
    while surplus > 0:
        candidates = [i for i in range(1, number_of) if counts[i] < largest] or [i for i in range(1, number_of) if counts[i] < bound]
        mass, remaining = sum([portions[i] for i in candidates]), surplus
        for i in candidates:
            more = min(bound - counts[i], max(1, remaining * portions[i] // mass), surplus)
            counts[i] = counts[i] + more
            surplus = surplus - more
    return np.array(counts)


def centred(rng, dims, scale, bound, split=(), held_as=jnp.bfloat16):
    gain = steps_of(rng, dims, split, -0.22, 0.18) if split else 1.0
    array = jax.random.normal(rng, dims, jnp.float32) * scale * gain
    return jnp.minimum(jnp.maximum(array, -bound), bound).astype(held_as)


def setup_inputs(seed: int = 0) -> dict:
    splits = jax.random.split(jax.random.key(seed), 6)
    tokens = centred(splits[0], (TOKENS, D), 1.0, 6.0, ((0, 32),))
    route_ids_keys = jax.random.split(jax.random.fold_in(splits[1], 1), TOKENS // TOK_DEV)
    route_ids_turns = jax.random.permutation(jax.random.fold_in(splits[1], 3), TOKENS // TOK_DEV)
    route_ids = jax.vmap(lambda own, number: deal_out(jax.random.fold_in(splits[1], 2), own, number, TOK_DEV, NROUTE, TOP, CAP, 2))(route_ids_keys, route_ids_turns).reshape((TOKENS, TOP))
    whiten = centred(splits[2], (EXPERTS, D, D), D ** -0.5, 0.09375, ((0, 8), (1, 32)))
    deltas = centred(splits[3], (EXPERTS, D, H), 1.0, 6.0, ((0, 8), (1, 32)))
    basis = centred(splits[4], (D, R), D ** -0.5, 0.09375, ((0, 8),))
    return dict(tokens=tokens, route_ids=route_ids, whiten=whiten, deltas=deltas, basis=basis)


def reference(tokens, route_ids, whiten, deltas, basis):
    scale = NROUTE / (TOP * TOKENS)
    expert_ids = jnp.arange(GRAM_EXP, dtype=jnp.int32)
    hits = jnp.any(route_ids[:, :, None] == expert_ids[None, None, :], axis=1)
    hit = hits.astype(jnp.bfloat16)
    grams = []
    for index in range(GRAM_EXP):
        weighted = tokens * hit[:, index:index + 1]
        grams.append(jnp.dot(weighted.T, tokens, preferred_element_type=jnp.float32) * scale)
    gram = jnp.stack(grams, axis=1)

    def one_expert(pair):
        factor, delta = pair
        whitened = jnp.dot(factor, basis, preferred_element_type=jnp.float32).astype(jnp.bfloat16)
        return jnp.dot(whitened.T, delta, preferred_element_type=jnp.float32)

    stacked = lax.map(one_expert, (whiten, deltas))
    coefficients = jnp.transpose(stacked, (1, 0, 2))
    basis_gram = jnp.einsum("keh,leh->kl", coefficients, coefficients, precision=lax.Precision.HIGHEST) / (EXPERTS * H)
    return gram, coefficients, basis_gram
```

```python
import jax
import jax.numpy as jnp
from jax import lax
from jax.experimental import pallas as pl
from jax.experimental.pallas import tpu as pltpu
from jax.sharding import Mesh
from jax.sharding import PartitionSpec as P

H = 1536
NROUTE = 128
TOP = 8
GRAM_EXP = 1
CAP = 128
EXPERTS = 16
TOK = ("x", "w", "c")
EXP = ("h", "y")
MESH = pl.DeviceIdType.MESH
F32 = jnp.float32
BF16 = jnp.bfloat16


class Ids:
    def __init__(self, **counts):
        self.total = 0
        for name, count in counts.items():
            setattr(self, name, self.total)
            self.total += count


S = Ids(
    loc=4, ya=4, fa=1, fb=1, yfa=4, yfb=4, wh=2, dx=4, dc=4, wx=4, tz=4, sc=1, co=16, e1=4, e2=4, e3=4, e4=1
)


def mm(a, b):
    return lax.dot_general(a, b, (((1,), (0,)), ((), ())), preferred_element_type=F32)


def mm_t(a, b):
    return lax.dot_general(a, b, (((0,), (0,)), ((), ())), preferred_element_type=F32)


def kernel(
    whiten, deltas, basis, coef_out, gram_out,
    bb, ww, dg, wg, ws, acc, tsum, ts, rz, spad, xs, st, cg, gs, er1, e2s, er2, er3, q4, er4, send, recv,
):
    x, w, c = lax.axis_index("x"), lax.axis_index("w"), lax.axis_index("c")
    h, y = lax.axis_index("h"), lax.axis_index("y")
    me, far = h * 4 + y, (1 - h) * 4 + y
    z = h * 4 + w
    up, down = lax.rem(z + 1, 8), lax.rem(z + 7, 8)
    half = pl.ds(pl.multiple_of(c * 384, 128), 384)

    def around(i, d):
        return lax.rem(i + d, 4)

    def remote(src, dst, s, r, dev):
        return pltpu.make_async_remote_copy(
            src_ref=src, dst_ref=dst, send_sem=send.at[s], recv_sem=recv.at[r], device_id=dev, device_id_type=MESH
        )

    def at_x(i):
        return (i, w, c, h, y)

    def at_w(i):
        return (x, i, c, h, y)

    def at_y(i):
        return (x, w, c, h, i)

    def at_z(i):
        return (x, lax.rem(i, 4), c, i // 4, y)

    other = (x, w, 1 - c, h, y)
    up_dev, down_dev = at_z(up), at_z(down)

    near_a, near_b = jnp.where(w == 0, me, far), jnp.where(w == 3, me, far)
    low, high = pl.ds(0, 256), pl.ds(256, 256)
    send_a = remote(bb.at[near_a, low], bb.at[near_a, low], S.fa, S.fa, down_dev)
    send_b = remote(bb.at[near_b, high], bb.at[near_b, high], S.fb, S.fb, up_dev)
    first_a = remote(basis.at[low, half], bb.at[me, low], S.fa, S.fa, down_dev)
    first_b = remote(basis.at[high, half], bb.at[me, high], S.fb, S.fb, up_dev)

    @pl.when(w == 0)
    def _():
        first_a.start()

    @pl.when(w == 3)
    def _():
        first_b.start()

    own_y = [remote(basis.at[:, half], bb.at[me], S.ya + d, S.ya + d, at_y(around(y, d))) for d in (1, 2, 3)]
    for copy in own_y:
        copy.start()
    mine = pl.multiple_of(c * 128, 128)
    wh = [remote(whiten.at[e], ww.at[pl.ds(e * 256 + mine, 128)], S.wh + e, S.wh + e, other) for e in (0, 1)]
    loc = [pltpu.make_async_copy(whiten.at[e], ww.at[pl.ds(e * 256 + mine, 128)], recv.at[S.loc + e]) for e in (0, 1)]
    loc.append(pltpu.make_async_copy(basis.at[:, half], bb.at[me], recv.at[S.loc + 2]))
    for copy in loc + wh:
        copy.start()

    def delta_part(i):
        return deltas.at[i // 2, :, pl.ds(pl.multiple_of(lax.rem(i, 2) * 768, 128), 768)]

    loc.append(pltpu.make_async_copy(delta_part(x), dg.at[x, c], recv.at[S.loc + 3]))
    loc[-1].start()
    dc = [remote(delta_part(x), dg.at[x, c], S.dc, S.dc, other)]
    dc[0].start()
    dx = [remote(delta_part(around(x, d)), dg.at[x, c], S.dx + d, S.dx + d, at_x(around(x, d))) for d in (1, 2, 3)]
    for copy in dx:
        copy.start()

    far_ya = [remote(bb.at[far, low], bb.at[far, low], S.yfa + d, S.yfa + d, at_y(around(y, d))) for d in (1, 2, 3)]
    far_yb = [remote(bb.at[far, high], bb.at[far, high], S.yfb + d, S.yfb + d, at_y(around(y, d))) for d in (1, 2, 3)]

    def take_a():
        send_a.wait_recv()

        @pl.when(w != 0)
        def _():
            send_a.start()

        for copy in far_ya:
            copy.start()

    def take_b():
        send_b.wait_recv()

        @pl.when(w != 3)
        def _():
            send_b.start()

        for copy in far_yb:
            copy.start()

    pl.when(w >= 2)(take_a)
    pl.when(w < 2)(take_b)

    for copy in loc[:3]:
        copy.wait()
    for copy in wh:
        copy.wait_recv()

    def add_block(block, first=False):
        part = mm(ww[:, pl.ds(pl.multiple_of(block * 512, 512), 512)], bb[block])
        acc[...] = part if first else acc[...] + part

    add_block(me, True)
    for d in (1, 2, 3):
        dx[d - 1].wait_recv()
        src = around(x, 4 - d)
        dc.append(remote(dg.at[src, c], dg.at[src, c], S.dc + d, S.dc + d, other))
        dc[-1].start()
    pl.when(w >= 2)(take_b)
    pl.when(w < 2)(take_a)

    for d in (1, 2, 3):
        own_y[d - 1].wait_recv()
        add_block(h * 4 + around(y, 4 - d))
    add_block(far)
    for d in (1, 2, 3):
        far_ya[d - 1].wait_recv()
        far_yb[d - 1].wait_recv()
        add_block((1 - h) * 4 + around(y, 4 - d))

    ws[...] = acc[...].astype(BF16)

    def expert_rows(i):
        return pl.ds(pl.multiple_of((i // 2) * 256, 256), 256)

    wx = [
        remote(ws.at[expert_rows(around(x, d))], wg.at[x], S.wx + d, S.wx + d, at_x(around(x, d))) for d in (1, 2, 3)
    ]
    for copy in wx:
        copy.start()
    loc[3].wait()
    for copy in dc:
        copy.wait_recv()

    def rows_of(i):
        return dg[i].reshape(256, 768)

    tsum[...] = mm_t(rows_of(x), ws[expert_rows(x)])
    for d in (1, 2, 3):
        wx[d - 1].wait_recv()
        src = around(x, 4 - d)
        tsum[...] += mm_t(rows_of(src), wg[src])

    ts[...] = tsum[...].astype(BF16).reshape(4, 192, 384)
    tz = [remote(ts.at[around(w, d)], rz.at[w], S.tz + d, S.tz + d, at_w(around(w, d))) for d in (2, 1, 3)]
    for copy in tz:
        copy.start()
    spad[...] = jnp.zeros_like(spad)
    total = tsum[pl.ds(pl.multiple_of(w * 192, 64), 192), :]
    for copy, d in zip(tz, (2, 1, 3)):
        copy.wait_recv()
        total += rz[around(w, 4 - d)].astype(F32)
    spad[pl.ds(pl.multiple_of(lax.rem(w, 2) * 64, 64), 192), :] = total
    xs[c] = total.astype(BF16)
    swap = remote(xs.at[c], xs.at[c], S.sc, S.sc, other)
    swap.start()
    st[...] = spad[...].T.reshape(16, 24, 256)

    def piece_dev(p):
        return (2 * c + p // 8, lax.rem(p, 8) // 2, lax.rem(p, 2), h, y)

    def is_me(dev):
        return (dev[0] == x) & (dev[1] == w) & (dev[2] == c)

    from_me = x * 4 + w

    def piece(p):
        return remote(st.at[p], cg.at[from_me], S.co + p, S.co + from_me, piece_dev(p))

    @pl.loop(0, 16)
    def _(p):
        here = is_me(piece_dev(p))

        @pl.when(here)
        def _():
            pltpu.make_async_copy(st.at[p], cg.at[from_me], recv.at[S.co + from_me]).start()

        @pl.when(jnp.logical_not(here))
        def _():
            piece(p).start()

    left = xs[c]
    swap.wait_recv()
    gram = jnp.concatenate([mm_t(left, xs[0]), mm_t(left, xs[1])], axis=1)
    for p in range(16):
        gs[p // 8, p % 2, (p % 8) // 2, 0:24, :] = gram[24 * p : 24 * p + 24].astype(BF16)

    def sum_dev(j, k):
        return (2 * c + j, w, k, h, y)

    e1 = {(j, k): remote(gs.at[j, k], er1.at[x], S.e1 + 2 * j + k, S.e1 + x, sum_dev(j, k)) for j in (0, 1) for k in (0, 1)}
    for (j, k), copy in e1.items():
        here = is_me(sum_dev(j, k))

        @pl.when(here)
        def _():
            pltpu.make_async_copy(gs.at[j, k], er1.at[x], recv.at[S.e1 + x]).start()

        @pl.when(jnp.logical_not(here))
        def _():
            copy.start()

    for i in range(4):
        pltpu.make_async_copy(er1.at[i], er1.at[i], recv.at[S.e1 + i]).wait()
        part = er1[i, :, 0:24, :].astype(F32)
        e2s[...] = part if i == 0 else e2s[...] + part
    e2 = [remote(e2s.at[around(w, d)], er2.at[w], S.e2 + d, S.e2 + d, at_w(around(w, d))) for d in (2, 1, 3)]
    for copy in e2:
        copy.start()
    row = e2s[w]
    for copy, d in zip(e2, (2, 1, 3)):
        copy.wait_recv()
        row += er2[around(w, 4 - d)]
    er3[y] = row
    e3 = [remote(er3.at[y], er3.at[y], S.e3 + d, S.e3 + d, at_y(around(y, d))) for d in (2, 1, 3)]
    for copy in e3:
        copy.start()

    for i in range(16):
        pltpu.make_async_copy(cg.at[i], cg.at[i], recv.at[S.co + i]).wait()
    for i in range(4):
        for pair in (0, 1):
            even, odd = cg[4 * i + 2 * pair], cg[4 * i + 2 * pair + 1]
            at = (i % 2) * 768 + pair * 384
            coef_out[i // 2, :, at : at + 128] = even[:, 0:128]
            coef_out[i // 2, :, at + 128 : at + 256] = even[:, 128:256] + odd[:, 0:128]
            coef_out[i // 2, :, at + 256 : at + 384] = odd[:, 128:256]

    for copy in e3:
        copy.wait_recv()
    q4[...] = (er3[0] + er3[1]) + (er3[2] + er3[3])
    e4 = remote(q4, er4, S.e4, S.e4, (x, w, c, 1 - h, y))
    e4.start()
    e4.wait_recv()
    gram_out[...] = (q4[...] + er4[...]) * (1.0 / (EXPERTS * H))

    for copy in own_y + wh + dc + dx + [send_a, send_b] + far_ya + far_yb + wx + tz + [swap] + e2 + e3 + [e4]:
        copy.wait_send()

    @pl.loop(0, 16)
    def _(p):
        @pl.when(jnp.logical_not(is_me(piece_dev(p))))
        def _():
            piece(p).wait_send()

    for (j, k), copy in e1.items():

        @pl.when(jnp.logical_not(is_me(sum_dev(j, k))))
        def _():
            copy.wait_send()


def coefficients_and_gram(whiten, deltas, basis):
    anywhere = pl.BlockSpec(memory_space=pl.ANY)
    vmem = pl.BlockSpec(memory_space=pltpu.VMEM)
    return pl.pallas_call(
        kernel,
        out_shape=(
            jax.ShapeDtypeStruct((2, 24, H), F32),
            jax.ShapeDtypeStruct((24, 768), F32),
        ),
        in_specs=[anywhere] * 3,
        out_specs=(vmem, vmem),
        scratch_shapes=[
            pltpu.VMEM((8, 512, 384), BF16),
            pltpu.VMEM((512, 4096), BF16),
            pltpu.VMEM((4, 2, 128, 768), BF16),
            pltpu.VMEM((4, 256, 384), BF16),
            pltpu.VMEM((512, 384), BF16),
            pltpu.VMEM((512, 384), F32),
            pltpu.VMEM((768, 384), F32),
            pltpu.VMEM((4, 192, 384), BF16),
            pltpu.VMEM((4, 192, 384), BF16),
            pltpu.VMEM((256, 384), F32),
            pltpu.VMEM((2, 192, 384), BF16),
            pltpu.VMEM((16, 24, 256), F32),
            pltpu.VMEM((16, 24, 256), F32),
            pltpu.VMEM((2, 2, 4, 32, 768), BF16),
            pltpu.VMEM((4, 4, 32, 768), BF16),
            pltpu.VMEM((4, 24, 768), F32),
            pltpu.VMEM((4, 24, 768), F32),
            pltpu.VMEM((4, 24, 768), F32),
            pltpu.VMEM((24, 768), F32),
            pltpu.VMEM((24, 768), F32),
            pltpu.SemaphoreType.DMA((S.total,)),
            pltpu.SemaphoreType.DMA((S.total,)),
        ],
        compiler_params=pltpu.CompilerParams(has_side_effects=True, vmem_limit_bytes=48 << 20),
        cost_estimate=pl.CostEstimate(flops=4 * 10**9, bytes_accessed=20 * 10**6, transcendentals=0),
    )(whiten, deltas, basis)


def split_up(x, dim, count):
    before, after = (x.shape[:dim], x.shape[dim + 1 :])
    return jnp.moveaxis(x.reshape(*before, count, -1, *after), dim, 0)


def joined_along(pieces, dim):
    lengths = list(pieces.shape[1:])
    lengths[dim] *= pieces.shape[0]
    return jnp.moveaxis(pieces, 0, dim).reshape(lengths)


def turned_blocks(pieces, axes, turns):
    inside = pieces.shape[1:]
    filled = pieces.reshape(*(lax.axis_size(a) for a in axes), *inside)
    for k in turns:
        filled = lax.all_to_all(filled, axes[k], k, k, tiled=True)
    return filled.reshape(-1, *inside)


def two_step_exchange(x, groups, turns, split_dim, concat_dim):
    count = lax.axis_size(groups[0]) * lax.axis_size(groups[1])
    pieces = split_up(x, split_dim, count)
    return joined_along(turned_blocks(pieces, groups, turns), concat_dim)


def routed_gram(tokens, route_ids):
    tok_count = lax.axis_size(TOK)
    exp_count = lax.axis_size(EXP)
    tok_rows, width = tokens.shape
    col_width = width // exp_count
    col_start = lax.axis_index(EXP) * col_width
    scale = NROUTE / (TOP * tok_rows * tok_count)
    expert_ids = jnp.arange(GRAM_EXP, dtype=jnp.int32)
    hits = jnp.any(route_ids[:, :, None] == expert_ids[None, None, :], axis=1)
    hit = hits.astype(jnp.bfloat16)
    order = jnp.argsort(1 - hits.T.astype(jnp.int32), axis=1, stable=True)[:, :CAP]
    slot_hit = jnp.take_along_axis(hit.T, order, axis=1)
    packed = tokens[order] * slot_hit[:, :, None]
    packed_cols = lax.dynamic_slice_in_dim(packed, col_start, col_width, 2)
    row_parts = two_step_exchange(packed, (("x", "w"), "c"), (1, 0), 2, 1)
    return (
        jnp.einsum(
            "gtd,gtc->dgc",
            row_parts,
            lax.all_gather(packed_cols, TOK, axis=1, tiled=True),
            preferred_element_type=jnp.float32,
        )
        * scale
    )


def shards(tokens, route_ids, whiten, deltas, basis):
    coefficients, basis_gram = coefficients_and_gram(whiten, deltas, basis)
    gram = routed_gram(tokens, route_ids)
    return gram, coefficients.transpose(1, 0, 2), basis_gram


def solution(mesh):
    torus = Mesh(mesh.devices.reshape(4, 4, 2, 2, 4), TOK + EXP)
    placed = (P(TOK, None), P(TOK, None), P(EXP, TOK, None), P(EXP, TOK, None), P(EXP, None))
    return jax.shard_map(
        shards,
        mesh=torus,
        in_specs=placed,
        out_specs=(P(TOK, None, EXP), P(TOK, EXP, None), P(TOK, None)),
        check_vma=False,
    )
```

```python
import jax
import jax.numpy as jnp
from jax import lax
from jax.experimental import pallas as pl
from jax.experimental.pallas import tpu as pltpu
from jax.sharding import Mesh
from jax.sharding import PartitionSpec as P

H = 1536
NROUTE = 128
TOP = 8
TOKENS = 24576
EXPERTS = 16
TOK = ("x", "w", "c")
EXP = ("h", "y")
MESH = pl.DeviceIdType.MESH
F32 = jnp.float32
BF16 = jnp.bfloat16


class Ids:
    def __init__(self, **counts):
        self.total = 0
        for name, count in counts.items():
            setattr(self, name, self.total)
            self.total += count


S = Ids(
    loc=16, fa=3, fb=3, yo=12, xo=12, yfa=12, yfb=12, wh=2, dx=4, dc=4, wx=12, tz=12, sc=3, co=16,
    e1=4, e2=4, e3=4, e4=1, gd=8, gc=4, gr=4, gy=4, gz=4,
)
PARTS = 3


def mm(a, b):
    return lax.dot_general(a, b, (((1,), (0,)), ((), ())), preferred_element_type=F32)


def mm_t(a, b):
    return lax.dot_general(a, b, (((0,), (0,)), ((), ())), preferred_element_type=F32)


def kernel(
    tokens, route_ids, whiten, deltas, basis, routed_out, coef_out, gram_out,
    tk, ids, pd, pc, gy, gc, gp, gx, gr,
    bb, xq, ww, dg, dt, wg, ws, acc, tsum, ts, rz, spad, xs, st, cg, gs, er1, e2s, e2b, er2, er3, q4, er4, send, recv,
):
    x, w, c = lax.axis_index("x"), lax.axis_index("w"), lax.axis_index("c")
    h, y = lax.axis_index("h"), lax.axis_index("y")
    me, far = h * 4 + y, (1 - h) * 4 + y
    z = h * 4 + w
    up, down = lax.rem(z + 1, 8), lax.rem(z + 7, 8)
    parts = range(PARTS)
    sent = []

    def around(i, d):
        return lax.rem(i + d, 4)

    def remote(src, dst, s, r, dev):
        return pltpu.make_async_remote_copy(
            src_ref=src, dst_ref=dst, send_sem=send.at[s], recv_sem=recv.at[r], device_id=dev, device_id_type=MESH
        )

    def start(copies):
        for copy in copies:
            copy.start()
        sent.extend(copies)
        return copies

    def arrive(copies):
        for copy in copies:
            copy.wait_recv()

    def local(src, dst, n):
        copy = pltpu.make_async_copy(src, dst, recv.at[S.loc + n])
        copy.start()
        return copy

    def at_x(i):
        return (i, w, c, h, y)

    def at_w(i):
        return (x, i, c, h, y)

    def at_y(i):
        return (x, w, c, h, i)

    def at_z(i):
        return (x, lax.rem(i, 4), c, i // 4, y)

    other = (x, w, 1 - c, h, y)
    up_dev, down_dev = at_z(up), at_z(down)
    opposite = (x, w, c, 1 - h, y)

    def columns(at, size):
        return pl.ds(pl.multiple_of(at, 128), size)

    mine = pl.multiple_of(c * 128, 128)
    basis_in = [local(basis.at[:, columns(c * 384 + 128 * n, 128)], bb.at[n, me], n) for n in parts]
    whiten_in = [local(whiten.at[e], ww.at[pl.ds(e * 256 + mine, 128)], 3 + e) for e in (0, 1)]
    ids_in = local(route_ids, ids, 5)

    def delta_part(i):
        return deltas.at[i // 2, :, columns(lax.rem(i, 2) * 768, 768)]

    delta_in = local(delta_part(x), dg.at[x, c], 6)
    token_in = [
        local(tokens.at[:, columns(1024 * i + 256 * y, 256)], tk.at[:, 256 * i : 256 * i + 256], 7 + i)
        for i in range(4)
    ]
    token_in.append(local(tokens.at[:, columns(512 * me, 512)], tk.at[:, 1024:1536], 11))

    barrier = pltpu.get_barrier_semaphore()
    friends = [(around(x, d), w, lax.rem(c + k, 2), h, y) for d in range(4) for k in (0, 1) if d or k]
    friends += [at_y(around(y, d)) for d in (1, 2, 3)] + [at_w(around(w, d)) for d in (1, 2, 3)] + [opposite]
    for dev in friends:
        pl.semaphore_signal(barrier, inc=1, device_id=dev, device_id_type=MESH)

    @pl.when(w == 0)
    def _():
        pl.semaphore_signal(barrier, inc=1, device_id=down_dev, device_id_type=MESH)

    @pl.when(w == 3)
    def _():
        pl.semaphore_signal(barrier, inc=1, device_id=up_dev, device_id_type=MESH)

    pl.semaphore_wait(barrier, len(friends) + jnp.where((w == 0) | (w == 3), 1, 0))

    near_a, near_b = jnp.where(w == 0, me, far), jnp.where(w == 3, me, far)
    low, high = pl.ds(0, 256), pl.ds(256, 256)
    send_a = [remote(bb.at[n, near_a, low], bb.at[n, near_a, low], S.fa + n, S.fa + n, down_dev) for n in parts]
    send_b = [remote(bb.at[n, near_b, high], bb.at[n, near_b, high], S.fb + n, S.fb + n, up_dev) for n in parts]
    for copy in basis_in:
        copy.wait()

    quarter = pl.ds(pl.multiple_of(x * 128, 128), 128)
    own_y = [
        [remote(bb.at[n, me, quarter], xq.at[n, x, d - 1], S.yo + 4 * n + d, S.yo + 4 * n + d, at_y(around(y, d))) for d in (1, 2, 3)]
        for n in parts
    ]
    own_x = [
        [remote(xq.at[n, x], xq.at[n, x], S.xo + 4 * n + d, S.xo + 4 * n + d, at_x(around(x, d))) for d in (1, 2, 3)]
        for n in parts
    ]
    for n in parts:

        @pl.when(w == 0)
        def _():
            send_a[n].start()

        @pl.when(w == 3)
        def _():
            send_b[n].start()

        start(own_y[n])

    wh = start([remote(whiten.at[e], ww.at[pl.ds(e * 256 + mine, 128)], S.wh + e, S.wh + e, other) for e in (0, 1)])
    dc = start([remote(delta_part(x), dg.at[x, c], S.dc, S.dc, other)])

    far_a = [
        [remote(bb.at[n, far, low], bb.at[n, far, low], S.yfa + 4 * n + d, S.yfa + 4 * n + d, at_y(around(y, d))) for d in (1, 2, 3)]
        for n in parts
    ]
    far_b = [
        [remote(bb.at[n, far, high], bb.at[n, far, high], S.yfb + 4 * n + d, S.yfb + 4 * n + d, at_y(around(y, d))) for d in (1, 2, 3)]
        for n in parts
    ]

    def take_a():
        for n in parts:
            send_a[n].wait_recv()

            @pl.when(w != 0)
            def _():
                send_a[n].start()

            for copy in far_a[n]:
                copy.start()

    def take_b():
        for n in parts:
            send_b[n].wait_recv()

            @pl.when(w != 3)
            def _():
                send_b[n].start()

            for copy in far_b[n]:
                copy.start()

    for n in parts:
        arrive(own_y[n])
        start(own_x[n])
        if n == 0:
            dx = start(
                [remote(delta_part(around(x, d)), dg.at[x, c], S.dx + d, S.dx + d, at_x(around(x, d))) for d in (1, 2, 3)]
            )
    pl.when(w >= 2)(take_a)
    pl.when(w < 2)(take_b)

    ids_in.wait()
    hit = jnp.max(jnp.where(ids[...] == 0, 1.0, 0.0), axis=0, keepdims=True)
    hits = jnp.broadcast_to(hit, (8, 768)).astype(BF16)
    earlier = lax.broadcasted_iota(jnp.int32, (768, 768), 0) <= lax.broadcasted_iota(jnp.int32, (768, 768), 1)
    place = mm(hits, jnp.where(earlier, 1.0, 0.0).astype(BF16))[0:1]
    place = jnp.broadcast_to(jnp.where(hit > 0.0, place, 0.0), (128, 768))
    slot = (lax.broadcasted_iota(jnp.int32, (128, 768), 0) + 1).astype(F32)
    pick = jnp.where(place == slot, 1.0, 0.0).astype(BF16)

    pl.when(w >= 2)(take_b)
    pl.when(w < 2)(take_a)
    sent.extend(send_a + send_b + sum(far_a, []) + sum(far_b, []))

    for copy in token_in:
        copy.wait()
    mine8 = 2 * x + c
    for n in range(4):
        part = mm(pick, tk[:, 256 * n : 256 * n + 256]).astype(BF16)
        pd[n, 0] = part[:, 0:128]
        pd[n, 1] = part[:, 128:256]
    pc[...] = mm(pick, tk[:, 1024:1536]).astype(BF16)
    gy[y, mine8] = pd[x, c]
    gc[mine8] = pc[...]

    delta_in.wait()
    for d in (1, 2, 3):
        dx[d - 1].wait_recv()
        src = around(x, 4 - d)
        dc += start([remote(dg.at[src, c], dg.at[src, c], S.dc + d, S.dc + d, other)])
    for copy in whiten_in:
        copy.wait()
    arrive(wh)
    arrive(dc)
    for i in range(4):
        dt[:, 256 * i : 256 * i + 256] = dg[i].reshape(256, 768).T

    def factor(block):
        return ww[:, columns(block * 512, 512)]

    def expert_rows(i):
        return pl.ds(pl.multiple_of((i // 2) * 256, 256), 256)

    def whitened(n):
        total = mm(factor(me), bb[n, me]) + mm(factor(far), bb[n, far])
        arrive(own_x[n])
        for d in (1, 2, 3):
            block = jnp.concatenate([xq[n, i, d - 1] for i in range(4)], axis=0)
            total += mm(factor(h * 4 + around(y, 4 - d)), block)
        for d in (1, 2, 3):
            from_y = (1 - h) * 4 + around(y, 4 - d)
            far_a[n][d - 1].wait_recv()
            far_b[n][d - 1].wait_recv()
            total += mm(factor(from_y), bb[n, from_y])
        ws[n] = total.astype(BF16)
        wg[n, x] = ws[n, expert_rows(x)]
        return start(
            [
                remote(ws.at[n, expert_rows(around(x, d))], wg.at[n, x], S.wx + 4 * n + d, S.wx + 4 * n + d, at_x(around(x, d)))
                for d in (1, 2, 3)
            ]
        )

    def hidden(n, wx):
        arrive(wx)
        tsum[n] = mm(dt[...], wg[n].reshape(1024, 128))
        ts[n] = tsum[n].astype(BF16).reshape(4, 192, 128)
        return start(
            [
                remote(ts.at[n, around(w, d)], rz.at[n, w], S.tz + 4 * n + d, S.tz + 4 * n + d, at_w(around(w, d)))
                for d in (2, 1, 3)
            ]
        )

    wx0 = whitened(0)
    wx1 = whitened(1)
    tz = [hidden(0, wx0)]
    wx2 = whitened(2)
    rows8 = start(
        [
            remote(
                pd.at[around(x, d), lax.rem(c + k, 2)], gy.at[y, mine8], S.gd + 2 * d + k, S.gd + 2 * d + k,
                (around(x, d), w, lax.rem(c + k, 2), h, y),
            )
            for d in range(4) for k in (0, 1) if d or k
        ]
    )
    cols = start([remote(pc, gc.at[mine8], S.gc + d, S.gc + d, at_x(around(x, d))) for d in (1, 2, 3)])
    cols_c = start([remote(pc, gc.at[mine8], S.gr, S.gr, other)])
    tz.append(hidden(1, wx1))
    tz.append(hidden(2, wx2))

    spad[...] = jnp.zeros_like(spad)
    swap = []
    for n in parts:
        total = tsum[n, pl.ds(pl.multiple_of(w * 192, 64), 192), :]
        for copy, d in zip(tz[n], (2, 1, 3)):
            copy.wait_recv()
            total += rz[n, around(w, 4 - d)].astype(F32)
        spad[pl.ds(pl.multiple_of(lax.rem(w, 2) * 64, 64), 192), 128 * n : 128 * n + 128] = total
        xs[c, n] = total.astype(BF16)
        swap += start([remote(xs.at[c, n], xs.at[c, n], S.sc + n, S.sc + n, other)])
    st[...] = spad[...].T.reshape(16, 24, 256)

    def piece_dev(p):
        return (2 * c + p // 8, lax.rem(p, 8) // 2, lax.rem(p, 2), h, y)

    def is_me(dev):
        return (dev[0] == x) & (dev[1] == w) & (dev[2] == c)

    from_me = x * 4 + w

    def piece(p):
        return remote(st.at[p], cg.at[from_me], S.co + p, S.co + from_me, piece_dev(p))

    @pl.loop(0, 16)
    def _(p):
        here = is_me(piece_dev(p))

        @pl.when(here)
        def _():
            pltpu.make_async_copy(st.at[p], cg.at[from_me], recv.at[S.co + from_me]).start()

        @pl.when(jnp.logical_not(here))
        def _():
            piece(p).start()

    arrive(swap)

    def wide(i):
        return jnp.concatenate([xs[i, n] for n in parts], axis=1)

    left = wide(c)
    for half in (0, 1):
        gram = mm_t(left, wide(half))
        for p in range(16):
            gs[p // 8, p % 2, (p % 8) // 2, :, 384 * half : 384 * half + 384] = gram[24 * p : 24 * p + 24].astype(BF16)

    def sum_dev(j, k):
        return (2 * c + j, w, k, h, y)

    e1 = {
        (j, k): remote(gs.at[j, k], er1.at[x], S.e1 + 2 * j + k, S.e1 + x, sum_dev(j, k)) for j in (0, 1) for k in (0, 1)
    }
    for (j, k), copy in e1.items():
        here = is_me(sum_dev(j, k))

        @pl.when(here)
        def _():
            pltpu.make_async_copy(gs.at[j, k], er1.at[x], recv.at[S.e1 + x]).start()

        @pl.when(jnp.logical_not(here))
        def _():
            copy.start()

    arrive(rows8)
    gy_all = start([remote(gy.at[y], gy.at[y], S.gy + d, S.gy + d, at_y(around(y, d))) for d in (1, 2, 3)])
    for d in (1, 2, 3):
        cols[d - 1].wait_recv()
        src = 2 * around(x, 4 - d) + c
        cols_c += start([remote(gc.at[src], gc.at[src], S.gr + d, S.gr + d, other)])

    for i in range(4):
        pltpu.make_async_copy(er1.at[i], er1.at[i], recv.at[S.e1 + i]).wait()
        part = er1[i].astype(F32)
        e2s[...] = part if i == 0 else e2s[...] + part
    e2b[...] = e2s[...].astype(BF16)
    e2 = start([remote(e2b.at[around(w, d)], er2.at[w], S.e2 + d, S.e2 + d, at_w(around(w, d))) for d in (2, 1, 3)])

    arrive(cols_c)
    arrive(gy_all)
    for i in range(4):
        gp[i] = mm_t(gy[i].reshape(1024, 128), gc[...].reshape(1024, 512))
    gx[...] = gp[...].astype(BF16)
    gz = start([remote(gx.at[around(w, d)], gr.at[w], S.gz + d, S.gz + d, at_w(around(w, d))) for d in (2, 1, 3)])

    row = e2s[w]
    for copy, d in zip(e2, (2, 1, 3)):
        copy.wait_recv()
        row += er2[around(w, 4 - d)].astype(F32)
    er3[y] = row
    e3 = start([remote(er3.at[y], er3.at[y], S.e3 + d, S.e3 + d, at_y(around(y, d))) for d in (2, 1, 3)])

    for i in range(16):
        pltpu.make_async_copy(cg.at[i], cg.at[i], recv.at[S.co + i]).wait()
    for i in range(4):
        for pair in (0, 1):
            even, odd = cg[4 * i + 2 * pair], cg[4 * i + 2 * pair + 1]
            at = (i % 2) * 768 + pair * 384
            coef_out[i // 2, :, at : at + 128] = even[:, 0:128]
            coef_out[i // 2, :, at + 128 : at + 256] = even[:, 128:256] + odd[:, 0:128]
            coef_out[i // 2, :, at + 256 : at + 384] = odd[:, 128:256]

    arrive(e3)
    q4[...] = (er3[0] + er3[1]) + (er3[2] + er3[3])
    e4 = start([remote(q4, er4, S.e4, S.e4, opposite)])
    routed = gp[w]
    for copy, d in zip(gz, (2, 1, 3)):
        copy.wait_recv()
        routed += gr[around(w, 4 - d)].astype(F32)
    routed_out[...] = routed * (NROUTE / (TOP * TOKENS))
    arrive(e4)
    gram_out[...] = (q4[...] + er4[...]) * (1.0 / (EXPERTS * H))

    for copy in sent:
        copy.wait_send()

    @pl.loop(0, 16)
    def _(p):
        @pl.when(jnp.logical_not(is_me(piece_dev(p))))
        def _():
            piece(p).wait_send()

    for (j, k), copy in e1.items():

        @pl.when(jnp.logical_not(is_me(sum_dev(j, k))))
        def _():
            copy.wait_send()


def whole(tokens, route_ids, whiten, deltas, basis):
    in_hbm = pl.BlockSpec(memory_space=pltpu.HBM)
    vmem = pl.BlockSpec(memory_space=pltpu.VMEM)
    return pl.pallas_call(
        kernel,
        out_shape=(
            jax.ShapeDtypeStruct((128, 512), F32),
            jax.ShapeDtypeStruct((2, 24, H), F32),
            jax.ShapeDtypeStruct((24, 768), F32),
        ),
        in_specs=[in_hbm] * 5,
        out_specs=(vmem, vmem, vmem),
        scratch_shapes=[
            pltpu.VMEM((768, 1536), BF16),
            pltpu.VMEM((8, 768), jnp.int32),
            pltpu.VMEM((4, 2, 128, 128), BF16),
            pltpu.VMEM((128, 512), BF16),
            pltpu.VMEM((4, 8, 128, 128), BF16),
            pltpu.VMEM((8, 128, 512), BF16),
            pltpu.VMEM((4, 128, 512), F32),
            pltpu.VMEM((4, 128, 512), BF16),
            pltpu.VMEM((4, 128, 512), BF16),
            pltpu.VMEM((PARTS, 8, 512, 128), BF16),
            pltpu.VMEM((PARTS, 4, 3, 128, 128), BF16),
            pltpu.VMEM((512, 4096), BF16),
            pltpu.VMEM((4, 2, 128, 768), BF16),
            pltpu.VMEM((768, 1024), BF16),
            pltpu.VMEM((PARTS, 4, 256, 128), BF16),
            pltpu.VMEM((PARTS, 512, 128), BF16),
            pltpu.VMEM((512, 128), F32),
            pltpu.VMEM((PARTS, 768, 128), F32),
            pltpu.VMEM((PARTS, 4, 192, 128), BF16),
            pltpu.VMEM((PARTS, 4, 192, 128), BF16),
            pltpu.VMEM((256, 384), F32),
            pltpu.VMEM((2, PARTS, 192, 128), BF16),
            pltpu.VMEM((16, 24, 256), F32),
            pltpu.VMEM((16, 24, 256), F32),
            pltpu.VMEM((2, 2, 4, 24, 768), BF16),
            pltpu.VMEM((4, 4, 24, 768), BF16),
            pltpu.VMEM((4, 24, 768), F32),
            pltpu.VMEM((4, 24, 768), BF16),
            pltpu.VMEM((4, 24, 768), BF16),
            pltpu.VMEM((4, 24, 768), F32),
            pltpu.VMEM((24, 768), F32),
            pltpu.VMEM((24, 768), F32),
            pltpu.SemaphoreType.DMA((S.total,)),
            pltpu.SemaphoreType.DMA((S.total,)),
        ],
        compiler_params=pltpu.CompilerParams(collective_id=0, has_side_effects=True, vmem_limit_bytes=52 << 20),
        cost_estimate=pl.CostEstimate(flops=4 * 10**9, bytes_accessed=20 * 10**6, transcendentals=0),
    )(tokens, route_ids, whiten, deltas, basis)


def shards(tokens, route_ids, whiten, deltas, basis):
    gram, coefficients, basis_gram = whole(tokens, route_ids.T, whiten, deltas, basis)
    return gram[:, None, :], coefficients.transpose(1, 0, 2), basis_gram


def solution(mesh):
    torus = Mesh(mesh.devices.reshape(4, 4, 2, 2, 4), TOK + EXP)
    placed = (P(TOK, None), P(TOK, None), P(EXP, TOK, None), P(EXP, TOK, None), P(EXP, None))
    return jax.shard_map(
        shards,
        mesh=torus,
        in_specs=placed,
        out_specs=(P(TOK, None, EXP), P(TOK, EXP, None), P(TOK, None)),
        check_vma=False,
    )
```

```python
import jax
import jax.numpy as jnp
from jax import lax
from jax.experimental import pallas as pl
from jax.experimental.pallas import tpu as pltpu
from jax.sharding import Mesh
from jax.sharding import PartitionSpec as P

H = 1536
NROUTE = 128
TOP = 8
TOKENS = 24576
EXPERTS = 16
TOK = ("x", "w", "c")
EXP = ("h", "y")
MESH = pl.DeviceIdType.MESH
F32 = jnp.float32
BF16 = jnp.bfloat16


class Ids:
    def __init__(self, **counts):
        self.total = 0
        for name, count in counts.items():
            setattr(self, name, self.total)
            self.total += count


S = Ids(
    loc=16, zq=3, fx=12, yf=12, yo=12, xo=12, wh=2, dx=4, dc=4, wx=12, tz=12, sl=12, sr=8, co=16,
    e2=32, e3=8, gd=8, gc=4, gr=4, gy=4, gz=4,
)
PARTS = 3


def mm(a, b):
    return lax.dot_general(a, b, (((1,), (0,)), ((), ())), preferred_element_type=F32)


def mm_t(a, b):
    return lax.dot_general(a, b, (((0,), (0,)), ((), ())), preferred_element_type=F32)


def kernel(
    tokens, route_ids, whiten, deltas, basis, routed_out, coef_out, gram_out,
    tk, ids, pd, pc, gy, gc, gp, gx, gr,
    bb, xq, ww, dg, dt, wg, ws, acc, tsum, ts, rz, spad, sx, rx, g2, st, cg, e2b, er2, q4, er3, send, recv,
):
    x, w, c = lax.axis_index("x"), lax.axis_index("w"), lax.axis_index("c")
    h, y = lax.axis_index("h"), lax.axis_index("y")
    me, far = h * 4 + y, (1 - h) * 4 + y
    parts = range(PARTS)
    sent = []

    def around(i, d):
        return lax.rem(i + d, 4)

    def remote(src, dst, s, r, dev):
        return pltpu.make_async_remote_copy(
            src_ref=src, dst_ref=dst, send_sem=send.at[s], recv_sem=recv.at[r], device_id=dev, device_id_type=MESH
        )

    def start(copies):
        for copy in copies:
            copy.start()
        sent.extend(copies)
        return copies

    def arrive(copies):
        for copy in copies:
            copy.wait_recv()

    def local(src, dst, n):
        copy = pltpu.make_async_copy(src, dst, recv.at[S.loc + n])
        copy.start()
        return copy

    def at_x(i):
        return (i, w, c, h, y)

    def at_w(i):
        return (x, i, c, h, y)

    def at_y(i):
        return (x, w, c, h, i)

    other = (x, w, 1 - c, h, y)
    opposite = (x, w, c, 1 - h, y)

    def columns(at, size):
        return pl.ds(pl.multiple_of(at, 128), size)

    mine = pl.multiple_of(c * 128, 128)
    basis_in = [local(basis.at[:, columns(c * 384 + 128 * n, 128)], bb.at[n, me], n) for n in parts]
    whiten_in = [local(whiten.at[e], ww.at[pl.ds(e * 256 + mine, 128)], 3 + e) for e in (0, 1)]
    ids_in = local(route_ids, ids, 5)

    def delta_part(i):
        return deltas.at[i // 2, :, columns(lax.rem(i, 2) * 768, 768)]

    delta_in = local(delta_part(x), dg.at[x, c], 6)
    token_in = [
        local(tokens.at[:, columns(1024 * y, 1024)], tk.at[:, 0:1024], 7),
        local(tokens.at[:, columns(512 * me, 512)], tk.at[:, 1024:1536], 8),
    ]

    barrier = pltpu.get_barrier_semaphore()
    friends = [(around(x, d), w, lax.rem(c + k, 2), h, y) for d in range(4) for k in (0, 1) if d or k]
    friends += [at_y(around(y, d)) for d in (1, 2, 3)] + [at_w(around(w, d)) for d in (1, 2, 3)] + [opposite]
    for dev in friends:
        pl.semaphore_signal(barrier, inc=1, device_id=dev, device_id_type=MESH)

    ids_in.wait()
    hit = jnp.max(jnp.where(ids[...] == 0, 1.0, 0.0), axis=0, keepdims=True)
    hits = jnp.broadcast_to(hit, (8, 768)).astype(BF16)
    earlier = lax.broadcasted_iota(jnp.int32, (768, 768), 0) <= lax.broadcasted_iota(jnp.int32, (768, 768), 1)
    place = mm(hits, jnp.where(earlier, 1.0, 0.0).astype(BF16))[0:1]
    place = jnp.broadcast_to(jnp.where(hit > 0.0, place, 0.0), (128, 768))
    slot = (lax.broadcasted_iota(jnp.int32, (128, 768), 0) + 1).astype(F32)
    pick = jnp.where(place == slot, 1.0, 0.0).astype(BF16)

    for copy in token_in:
        copy.wait()
    mine8 = 2 * w + c
    for n in range(4):
        part = mm(pick, tk[:, 256 * n : 256 * n + 256]).astype(BF16)
        pd[n, 0] = part[:, 0:128]
        pd[n, 1] = part[:, 128:256]
    pc[...] = mm(pick, tk[:, 1024:1536]).astype(BF16)
    gy[y, mine8] = pd[w, c]
    gc[mine8] = pc[...]

    pl.semaphore_wait(barrier, len(friends))

    quarter = pl.ds(pl.multiple_of(x * 128, 128), 128)
    zq = [remote(bb.at[n, me, quarter], bb.at[n, me, quarter], S.zq + n, S.zq + n, opposite) for n in parts]
    fx = [
        [remote(bb.at[n, far, quarter], bb.at[n, far, quarter], S.fx + 4 * n + d, S.fx + 4 * n + d, at_x(around(x, d))) for d in (2, 1, 3)]
        for n in parts
    ]
    yf = [
        [remote(bb.at[n, far], bb.at[n, far], S.yf + 4 * n + d, S.yf + 4 * n + d, at_y(around(y, d))) for d in (2, 1, 3)]
        for n in parts
    ]
    own_y = [
        [
            remote(
                bb.at[n, me] if n == 0 else bb.at[n, me, quarter],
                bb.at[n, me] if n == 0 else xq.at[n, x, d - 1],
                S.yo + 4 * n + d, S.yo + 4 * n + d, at_y(around(y, d)),
            )
            for d in (1, 2, 3)
        ]
        for n in parts
    ]
    own_x = [
        [remote(xq.at[n, x], xq.at[n, x], S.xo + 4 * n + d, S.xo + 4 * n + d, at_x(around(x, d))) for d in (2, 1, 3)]
        for n in parts
    ]
    for n in parts:
        basis_in[n].wait()
        start([zq[n]])
    for n in parts:
        start(own_y[n])
    wh = start([remote(whiten.at[e], ww.at[pl.ds(e * 256 + mine, 128)], S.wh + e, S.wh + e, other) for e in (0, 1)])
    dc = start([remote(delta_part(x), dg.at[x, c], S.dc, S.dc, other)])

    def arrived(dst, sem):
        pltpu.make_async_copy(dst, dst, recv.at[sem]).wait()

    def factor(at, size):
        return ww[:, columns(at, size)]

    for n in parts:
        arrived(bb.at[n, far, quarter], S.zq + n)
        start(fx[n])
    dx = start([remote(delta_part(around(x, d)), dg.at[x, c], S.dx + d, S.dx + d, at_x(around(x, d))) for d in (2, 1, 3)])
    for copy in whiten_in:
        copy.wait()
    arrive(wh)
    acc[0] = mm(factor(me * 512, 512), bb[0, me])
    for n in parts:
        for d in (2, 1, 3):
            arrived(bb.at[n, far, quarter], S.fx + 4 * n + d)
        start(yf[n])
        if n:
            arrive(own_y[n])
            start(own_x[n])
    for n in (1, 2):
        acc[n] = mm(factor(me * 512, 512), bb[n, me])

    rows8 = start(
        [
            remote(
                pd.at[around(w, d), lax.rem(c + k, 2)], gy.at[y, mine8], S.gd + 2 * d + k, S.gd + 2 * d + k,
                (x, around(w, d), lax.rem(c + k, 2), h, y),
            )
            for d in range(4) for k in (0, 1) if d or k
        ]
    )
    cols = start([remote(pc, gc.at[mine8], S.gc + d, S.gc + d, at_w(around(w, d))) for d in (1, 2, 3)])
    cols_c = start([remote(pc, gc.at[mine8], S.gr, S.gr, other)])

    for n in parts:
        acc[n] += mm(factor(far * 512, 512), bb[n, far])

    for d in (1, 2, 3):
        block = h * 4 + around(y, 4 - d)
        arrived(bb.at[0, block], S.yo + d)
        acc[0] += mm(factor(block * 512, 512), bb[0, block])

    delta_in.wait()
    for copy, d in zip(dx, (2, 1, 3)):
        copy.wait_recv()
        src = around(x, 4 - d)
        dc += start([remote(dg.at[src, c], dg.at[src, c], S.dc + d, S.dc + d, other)])

    def from_y(d):
        return (1 - h) * 4 + around(y, 4 - d)

    def expert_rows(i):
        return pl.ds(pl.multiple_of((i // 2) * 256, 256), 256)

    def whitened(n):
        total = acc[n]
        if n:
            arrive(own_x[n])
            for d in (1, 2, 3):
                block = jnp.concatenate([xq[n, i, d - 1] for i in range(4)], axis=0)
                total += mm(factor((h * 4 + around(y, 4 - d)) * 512, 512), block)
        for d in (2, 1, 3):
            arrived(bb.at[n, from_y(d)], S.yf + 4 * n + d)
            total += mm(factor(from_y(d) * 512, 512), bb[n, from_y(d)])
        ws[n] = total.astype(BF16)
        wg[n, x] = ws[n, expert_rows(x)]
        return start(
            [
                remote(ws.at[n, expert_rows(around(x, d))], wg.at[n, x], S.wx + 4 * n + d, S.wx + 4 * n + d, at_x(around(x, d)))
                for d in (2, 1, 3)
            ]
        )

    def hidden(n, wx):
        arrive(wx)
        tsum[n] = mm(dt[...], wg[n].reshape(1024, 128))
        ts[n] = tsum[n].astype(BF16).reshape(4, 192, 128)
        return start(
            [
                remote(ts.at[n, around(w, d)], rz.at[n, w], S.tz + 4 * n + d, S.tz + 4 * n + d, at_w(around(w, d)))
                for d in (2, 1, 3)
            ]
        )

    wx0 = whitened(0)
    arrive(dc)
    for i in range(4):
        dt[:, 256 * i : 256 * i + 256] = dg[i].reshape(256, 768).T
    wx1 = whitened(1)
    tz = [hidden(0, wx0)]
    wx2 = whitened(2)
    tz.append(hidden(1, wx1))
    tz.append(hidden(2, wx2))

    arrive(rows8)
    gy_all = start([remote(gy.at[y], gy.at[y], S.gy + d, S.gy + d, at_y(around(y, d))) for d in (1, 2, 3)])
    for d in (1, 2, 3):
        cols[d - 1].wait_recv()
        src = 2 * around(w, 4 - d) + c
        cols_c += start([remote(gc.at[src], gc.at[src], S.gr + d, S.gr + d, other)])

    spad[...] = jnp.zeros_like(spad)
    swap, rows = [], {}
    for n in parts:
        total = tsum[n, pl.ds(pl.multiple_of(w * 192, 64), 192), :]
        for copy, d in zip(tz[n], (2, 1, 3)):
            copy.wait_recv()
            total += rz[n, around(w, 4 - d)].astype(F32)
        sx[n, x] = total.astype(BF16)
        swap.append(
            start([remote(sx.at[n, x], sx.at[n, x], S.sl + 4 * n + d, S.sl + 4 * n + d, at_x(around(x, d))) for d in (2, 1, 3)])
        )
        for j in (0, 1):
            if 0 <= n - j <= 1:
                start([remote(sx.at[n, x], rx.at[n - j, x], S.sr + 2 * n + j, S.sr + 4 * (n - j) + x, (2 * c + j, w, 1 - c, h, y))])
        spad[pl.ds(pl.multiple_of(lax.rem(w, 2) * 64, 64), 192), 128 * n : 128 * n + 128] = total
    st[...] = spad[...].T.reshape(16, 24, 256)

    def piece_dev(p):
        return (2 * c + p // 8, lax.rem(p, 8) // 2, lax.rem(p, 2), h, y)

    def is_me(dev):
        return (dev[0] == x) & (dev[1] == w) & (dev[2] == c)

    from_me = x * 4 + w

    def piece(p):
        return remote(st.at[p], cg.at[from_me], S.co + p, S.co + from_me, piece_dev(p))

    @pl.loop(0, 16)
    def _(p):
        here = is_me(piece_dev(p))

        @pl.when(here)
        def _():
            pltpu.make_async_copy(st.at[p], cg.at[from_me], recv.at[S.co + from_me]).start()

        @pl.when(jnp.logical_not(here))
        def _():
            piece(p).start()

    for n in parts:
        for d in (2, 1, 3):
            arrived(sx.at[n, around(x, 4 - d)], S.sl + 4 * n + d)
    odd = lax.rem(x, 2)

    @pl.when(c == x // 2)
    def _():
        rx[...] = sx[pl.ds(odd, 2)]

    @pl.when(c != x // 2)
    def _():
        for r in (0, 1):
            for i in range(4):
                arrived(rx.at[r, i], S.sr + 4 * r + i)

    lhs = jnp.concatenate([rx[r].reshape(768, 128) for r in (0, 1)], axis=1)
    g2[...] = mm_t(lhs, jnp.concatenate([sx[n].reshape(768, 128) for n in parts], axis=1))
    gram = g2[pl.ds(pl.multiple_of(odd * 64, 64), 192), :]
    for p in range(8):
        for n in parts:
            e2b[3 * p + n] = gram[24 * p : 24 * p + 24, 128 * n : 128 * n + 128].astype(BF16)

    def exp_dev(i, core, e):
        return (x, i, core, e // 4, lax.rem(e, 4))

    from_here = w * 8 + me

    def sum_piece(p):
        i, core, e = p // 6, lax.rem(p // 3, 2), 3 * c + lax.rem(p, 3)
        return (i == w) & (core == c) & (e == me), remote(
            e2b.at[p], er2.at[from_here], S.e2 + p, S.e2 + from_here, exp_dev(i, core, e)
        )

    @pl.loop(0, 24)
    def _(p):
        here, copy = sum_piece(p)

        @pl.when(here)
        def _():
            pltpu.make_async_copy(e2b.at[p], er2.at[from_here], recv.at[S.e2 + from_here]).start()

        @pl.when(jnp.logical_not(here))
        def _():
            copy.start()

    arrive(cols_c)
    arrive(gy_all)
    for i in range(4):
        gp[i] = mm_t(gy[i].reshape(1024, 128), gc[...].reshape(1024, 512))
    gx[...] = gp[...].astype(BF16)
    gz = start([remote(gx.at[around(x, d)], gr.at[x], S.gz + d, S.gz + d, at_x(around(x, d))) for d in (2, 1, 3)])

    e3 = [remote(q4, er3.at[me], S.e3 + d, S.e3 + me, exp_dev(w, c, lax.rem(me + d, 8))) for d in range(1, 8)]

    @pl.when(me < 6)
    def _():
        row = None
        for i in range(32):
            arrived(er2.at[i], S.e2 + i)
        for i in range(32):
            part = er2[i].astype(F32)
            row = part if i == 0 else row + part
        q4[...] = row * (1.0 / (EXPERTS * H))
        pltpu.make_async_copy(q4, er3.at[me], recv.at[S.e3 + me]).start()
        for copy in e3:
            copy.start()

    for i in range(16):
        pltpu.make_async_copy(cg.at[i], cg.at[i], recv.at[S.co + i]).wait()
    for i in range(4):
        for pair in (0, 1):
            even, odd = cg[4 * i + 2 * pair], cg[4 * i + 2 * pair + 1]
            at = (i % 2) * 768 + pair * 384
            coef_out[i // 2, :, at : at + 128] = even[:, 0:128]
            coef_out[i // 2, :, at + 128 : at + 256] = even[:, 128:256] + odd[:, 0:128]
            coef_out[i // 2, :, at + 256 : at + 384] = odd[:, 128:256]

    routed = gp[x]
    for copy, d in zip(gz, (2, 1, 3)):
        copy.wait_recv()
        routed += gr[around(x, 4 - d)].astype(F32)
    routed_out[...] = routed * (NROUTE / (TOP * TOKENS))

    for i in range(6):
        arrived(er3.at[i], S.e3 + i)
        gram_out[:, 128 * i : 128 * i + 128] = er3[i]

    for copy in sent:
        copy.wait_send()

    @pl.loop(0, 16)
    def _(p):
        @pl.when(jnp.logical_not(is_me(piece_dev(p))))
        def _():
            piece(p).wait_send()


    @pl.loop(0, 24)
    def _(p):
        here, copy = sum_piece(p)

        @pl.when(jnp.logical_not(here))
        def _():
            copy.wait_send()

    @pl.when(me < 6)
    def _():
        for copy in e3:
            copy.wait_send()


def whole(tokens, route_ids, whiten, deltas, basis):
    in_hbm = pl.BlockSpec(memory_space=pltpu.HBM)
    vmem = pl.BlockSpec(memory_space=pltpu.VMEM)
    return pl.pallas_call(
        kernel,
        out_shape=(
            jax.ShapeDtypeStruct((128, 512), F32),
            jax.ShapeDtypeStruct((2, 24, H), F32),
            jax.ShapeDtypeStruct((24, 768), F32),
        ),
        in_specs=[in_hbm] * 5,
        out_specs=(vmem, vmem, vmem),
        scratch_shapes=[
            pltpu.VMEM((768, 1536), BF16),
            pltpu.VMEM((8, 768), jnp.int32),
            pltpu.VMEM((4, 2, 128, 128), BF16),
            pltpu.VMEM((128, 512), BF16),
            pltpu.VMEM((4, 8, 128, 128), BF16),
            pltpu.VMEM((8, 128, 512), BF16),
            pltpu.VMEM((4, 128, 512), F32),
            pltpu.VMEM((4, 128, 512), BF16),
            pltpu.VMEM((4, 128, 512), BF16),
            pltpu.VMEM((PARTS, 8, 512, 128), BF16),
            pltpu.VMEM((PARTS, 4, 3, 128, 128), BF16),
            pltpu.VMEM((512, 4096), BF16),
            pltpu.VMEM((4, 2, 128, 768), BF16),
            pltpu.VMEM((768, 1024), BF16),
            pltpu.VMEM((PARTS, 4, 256, 128), BF16),
            pltpu.VMEM((PARTS, 512, 128), BF16),
            pltpu.VMEM((PARTS, 512, 128), F32),
            pltpu.VMEM((PARTS, 768, 128), F32),
            pltpu.VMEM((PARTS, 4, 192, 128), BF16),
            pltpu.VMEM((PARTS, 4, 192, 128), BF16),
            pltpu.VMEM((256, 384), F32),
            pltpu.VMEM((PARTS, 4, 192, 128), BF16),
            pltpu.VMEM((2, 4, 192, 128), BF16),
            pltpu.VMEM((256, 384), F32),
            pltpu.VMEM((16, 24, 256), F32),
            pltpu.VMEM((16, 24, 256), F32),
            pltpu.VMEM((24, 24, 128), BF16),
            pltpu.VMEM((32, 24, 128), BF16),
            pltpu.VMEM((24, 128), F32),
            pltpu.VMEM((6, 24, 128), F32),
            pltpu.SemaphoreType.DMA((S.total,)),
            pltpu.SemaphoreType.DMA((S.total,)),
        ],
        compiler_params=pltpu.CompilerParams(collective_id=0, has_side_effects=True, vmem_limit_bytes=52 << 20),
        cost_estimate=pl.CostEstimate(flops=4 * 10**9, bytes_accessed=20 * 10**6, transcendentals=0),
    )(*(pltpu.with_memory_space_constraint(a, pltpu.HBM) for a in (tokens, route_ids, whiten, deltas, basis)))


def shards(tokens, route_ids, whiten, deltas, basis):
    gram, coefficients, basis_gram = whole(tokens, route_ids.T, whiten, deltas, basis)
    return gram[:, None, :], coefficients.transpose(1, 0, 2), basis_gram


def solution(mesh):
    torus = Mesh(mesh.devices.reshape(4, 4, 2, 2, 4), TOK + EXP)
    placed = (P(TOK, None), P(TOK, None), P(EXP, TOK, None), P(EXP, TOK, None), P(EXP, None))
    return jax.shard_map(
        shards,
        mesh=torus,
        in_specs=placed,
        out_specs=(P(TOK, None, EXP), P(TOK, EXP, None), P(TOK, None)),
        check_vma=False,
    )
```

```python
import jax
import jax.numpy as jnp
from jax import lax
from jax.experimental import pallas as pl
from jax.experimental.pallas import tpu as pltpu
from jax.sharding import Mesh
from jax.sharding import PartitionSpec as P

H = 1536
NROUTE = 128
TOP = 8
TOKENS = 24576
EXPERTS = 16
TOK = ("x", "w", "c")
EXP = ("h", "y")
MESH = pl.DeviceIdType.MESH
F32 = jnp.float32
BF16 = jnp.bfloat16


class Ids:
    def __init__(self, **counts):
        self.total = 0
        for name, count in counts.items():
            setattr(self, name, self.total)
            self.total += count


S = Ids(
    loc=16, zq=3, fx=12, yf=12, yo=12, xo=12, wh=2, dx=4, dc=4, wx=12, tz=12, sl=12, sr=8, co=16,
    e2=32, e3=8, gd=8, gc=4, gr=4, gy=4, gz=4,
)
PARTS = 3


def mm(a, b):
    return lax.dot_general(a, b, (((1,), (0,)), ((), ())), preferred_element_type=F32)


def mm_t(a, b):
    return lax.dot_general(a, b, (((0,), (0,)), ((), ())), preferred_element_type=F32)


def kernel(
    tokens, route_ids, whiten, deltas, basis, routed_out, coef_out, gram_out,
    tk, ids, pd, pc, gy, gc, gp, gx, gr,
    bb, xq, ww, dg, dt, wg, ws, acc, tsum, ts, rz, spad, sx, rx, g2, st, cg, e2b, er2, q4, er3, send, recv,
):
    x, w, c = lax.axis_index("x"), lax.axis_index("w"), lax.axis_index("c")
    h, y = lax.axis_index("h"), lax.axis_index("y")
    me, far = h * 4 + y, (1 - h) * 4 + y
    parts = range(PARTS)
    sent = []

    def around(i, d):
        return lax.rem(i + d, 4)

    def remote(src, dst, s, r, dev):
        return pltpu.make_async_remote_copy(
            src_ref=src, dst_ref=dst, send_sem=send.at[s], recv_sem=recv.at[r], device_id=dev, device_id_type=MESH
        )

    def start(copies):
        for copy in copies:
            copy.start()
        sent.extend(copies)
        return copies

    def arrive(copies):
        for copy in copies:
            copy.wait_recv()

    def local(src, dst, n):
        copy = pltpu.make_async_copy(src, dst, recv.at[S.loc + n])
        copy.start()
        return copy

    def at_x(i):
        return (i, w, c, h, y)

    def at_w(i):
        return (x, i, c, h, y)

    def at_y(i):
        return (x, w, c, h, i)

    other = (x, w, 1 - c, h, y)
    opposite = (x, 3 - w, c, 1 - h, y)

    def columns(at, size):
        return pl.ds(pl.multiple_of(at, 128), size)

    mine = pl.multiple_of(c * 128, 128)
    basis_in = [local(basis.at[:, columns(c * 384 + 128 * n, 128)], bb.at[n, me], n) for n in parts]
    whiten_in = [local(whiten.at[e], ww.at[pl.ds(e * 256 + mine, 128)], 3 + e) for e in (0, 1)]
    ids_in = local(route_ids, ids, 5)

    def delta_part(i):
        return deltas.at[i // 2, :, columns(lax.rem(i, 2) * 768, 768)]

    delta_in = local(delta_part(x), dg.at[x, c], 6)
    token_in = [
        local(tokens.at[:, columns(1024 * y, 1024)], tk.at[:, 0:1024], 7),
        local(tokens.at[:, columns(512 * me, 512)], tk.at[:, 1024:1536], 8),
    ]

    barrier = pltpu.get_barrier_semaphore()
    friends = [(around(x, d), w, lax.rem(c + k, 2), h, y) for d in range(4) for k in (0, 1) if d or k]
    friends += [at_y(around(y, d)) for d in (1, 2, 3)] + [at_w(around(w, d)) for d in (1, 2, 3)] + [opposite]
    for dev in friends:
        pl.semaphore_signal(barrier, inc=1, device_id=dev, device_id_type=MESH)

    pl.semaphore_wait(barrier, len(friends))

    quarter = pl.ds(pl.multiple_of(x * 128, 128), 128)
    zq = [remote(bb.at[n, me, quarter], bb.at[n, me, quarter], S.zq + n, S.zq + n, opposite) for n in parts]
    fx = [
        [remote(bb.at[n, far, quarter], bb.at[n, far, quarter], S.fx + 4 * n + d, S.fx + 4 * n + d, at_x(around(x, d))) for d in (2, 1, 3)]
        for n in parts
    ]
    yf = [
        [remote(bb.at[n, far], bb.at[n, far], S.yf + 4 * n + d, S.yf + 4 * n + d, at_y(around(y, d))) for d in (2, 1, 3)]
        for n in parts
    ]
    own_y = [
        [
            remote(
                bb.at[n, me] if n == 0 else bb.at[n, me, quarter],
                bb.at[n, me] if n == 0 else xq.at[n, x, d - 1],
                S.yo + 4 * n + d, S.yo + 4 * n + d, at_y(around(y, d)),
            )
            for d in (1, 2, 3)
        ]
        for n in parts
    ]
    own_x = [
        [remote(xq.at[n, x], xq.at[n, x], S.xo + 4 * n + d, S.xo + 4 * n + d, at_x(around(x, d))) for d in (2, 1, 3)]
        for n in parts
    ]
    for n in parts:
        basis_in[n].wait()
        start([zq[n]])
    for n in parts:
        start(own_y[n])
    wh = start([remote(whiten.at[e], ww.at[pl.ds(e * 256 + mine, 128)], S.wh + e, S.wh + e, other) for e in (0, 1)])
    dc = start([remote(delta_part(x), dg.at[x, c], S.dc, S.dc, other)])

    ids_in.wait()
    hit = jnp.max(jnp.where(ids[...] == 0, 1.0, 0.0), axis=0, keepdims=True)
    hits = jnp.broadcast_to(hit, (8, 768)).astype(BF16)
    earlier = lax.broadcasted_iota(jnp.int32, (768, 768), 0) <= lax.broadcasted_iota(jnp.int32, (768, 768), 1)
    place = mm(hits, jnp.where(earlier, 1.0, 0.0).astype(BF16))[0:1]
    place = jnp.broadcast_to(jnp.where(hit > 0.0, place, 0.0), (128, 768))
    slot = (lax.broadcasted_iota(jnp.int32, (128, 768), 0) + 1).astype(F32)
    pick = jnp.where(place == slot, 1.0, 0.0).astype(BF16)

    def arrived(dst, sem):
        pltpu.make_async_copy(dst, dst, recv.at[sem]).wait()

    def factor(at, size):
        return ww[:, columns(at, size)]

    for n in parts:
        arrived(bb.at[n, far, quarter], S.zq + n)
        start(fx[n])
    dx = start([remote(delta_part(around(x, d)), dg.at[x, c], S.dx + d, S.dx + d, at_x(around(x, d))) for d in (2, 1, 3)])
    for copy in token_in:
        copy.wait()
    mine8 = 2 * w + c
    for n in range(4):
        part = mm(pick, tk[:, 256 * n : 256 * n + 256]).astype(BF16)
        pd[n, 0] = part[:, 0:128]
        pd[n, 1] = part[:, 128:256]
    pc[...] = mm(pick, tk[:, 1024:1536]).astype(BF16)
    gy[y, mine8] = pd[w, c]
    gc[mine8] = pc[...]

    for copy in whiten_in:
        copy.wait()
    arrive(wh)
    acc[0] = mm(factor(me * 512, 512), bb[0, me])
    for n in parts:
        for d in (2, 1, 3):
            arrived(bb.at[n, far, quarter], S.fx + 4 * n + d)
        start(yf[n])
        if n == 1:
            arrive(own_y[n])
            start(own_x[n])
    for n in (1, 2):
        acc[n] = mm(factor(me * 512, 512), bb[n, me])

    rows8 = start(
        [
            remote(
                pd.at[around(w, d), lax.rem(c + k, 2)], gy.at[y, mine8], S.gd + 2 * d + k, S.gd + 2 * d + k,
                (x, around(w, d), lax.rem(c + k, 2), h, y),
            )
            for d in range(4) for k in (0, 1) if d or k
        ]
    )
    cols = start([remote(pc, gc.at[mine8], S.gc + d, S.gc + d, at_w(around(w, d))) for d in (1, 2, 3)])
    cols_c = start([remote(pc, gc.at[mine8], S.gr, S.gr, other)])

    for n in parts:
        acc[n] += mm(factor(far * 512, 512), bb[n, far])

    for d in (1, 2, 3):
        block = h * 4 + around(y, 4 - d)
        arrived(bb.at[0, block], S.yo + d)
        acc[0] += mm(factor(block * 512, 512), bb[0, block])

    delta_in.wait()
    for copy, d in zip(dx, (2, 1, 3)):
        copy.wait_recv()
        src = around(x, 4 - d)
        dc += start([remote(dg.at[src, c], dg.at[src, c], S.dc + d, S.dc + d, other)])

    def from_y(d):
        return (1 - h) * 4 + around(y, 4 - d)

    def expert_rows(i):
        return pl.ds(pl.multiple_of((i // 2) * 256, 256), 256)

    def whitened(n):
        total = acc[n]
        if n:
            arrive(own_x[n])
            for d in (1, 2, 3):
                block = jnp.concatenate([xq[n, i, d - 1] for i in range(4)], axis=0)
                total += mm(factor((h * 4 + around(y, 4 - d)) * 512, 512), block)
        for d in (2, 1, 3):
            arrived(bb.at[n, from_y(d)], S.yf + 4 * n + d)
            total += mm(factor(from_y(d) * 512, 512), bb[n, from_y(d)])
        ws[n] = total.astype(BF16)
        wg[n, x] = ws[n, expert_rows(x)]
        return start(
            [
                remote(ws.at[n, expert_rows(around(x, d))], wg.at[n, x], S.wx + 4 * n + d, S.wx + 4 * n + d, at_x(around(x, d)))
                for d in (2, 1, 3)
            ]
        )

    def hidden(n, wx):
        arrive(wx)
        tsum[n] = mm(dt[...], wg[n].reshape(1024, 128))
        ts[n] = tsum[n].astype(BF16).reshape(4, 192, 128)
        return start(
            [
                remote(ts.at[n, around(w, d)], rz.at[n, w], S.tz + 4 * n + d, S.tz + 4 * n + d, at_w(around(w, d)))
                for d in (2, 1, 3)
            ]
        )

    wx0 = whitened(0)
    arrive(own_y[2])
    start(own_x[2])
    arrive(dc)
    for i in range(4):
        dt[:, 256 * i : 256 * i + 256] = dg[i].reshape(256, 768).T
    wx1 = whitened(1)
    tz = [hidden(0, wx0)]
    wx2 = whitened(2)
    arrive(rows8)
    gy_all = start([remote(gy.at[y], gy.at[y], S.gy + d, S.gy + d, at_y(around(y, d))) for d in (1, 2, 3)])
    for d in (1, 2, 3):
        cols[d - 1].wait_recv()
        src = 2 * around(w, 4 - d) + c
        cols_c += start([remote(gc.at[src], gc.at[src], S.gr + d, S.gr + d, other)])

    tz.append(hidden(1, wx1))
    tz.append(hidden(2, wx2))

    spad[...] = jnp.zeros_like(spad)
    swap, rows = [], {}
    for n in parts:
        total = tsum[n, pl.ds(pl.multiple_of(w * 192, 64), 192), :]
        for copy, d in zip(tz[n], (2, 1, 3)):
            copy.wait_recv()
            total += rz[n, around(w, 4 - d)].astype(F32)
        sx[n, x] = total.astype(BF16)
        swap.append(
            start([remote(sx.at[n, x], sx.at[n, x], S.sl + 4 * n + d, S.sl + 4 * n + d, at_x(around(x, d))) for d in (2, 1, 3)])
        )
        for j in (0, 1):
            if 0 <= n - j <= 1:
                start([remote(sx.at[n, x], rx.at[n - j, x], S.sr + 2 * n + j, S.sr + 4 * (n - j) + x, (2 * c + j, w, 1 - c, h, y))])
        spad[pl.ds(pl.multiple_of(lax.rem(w, 2) * 64, 64), 192), 128 * n : 128 * n + 128] = total
    st[...] = spad[...].T.reshape(16, 24, 256)

    def piece_dev(p):
        return (2 * c + p // 8, lax.rem(p, 8) // 2, lax.rem(p, 2), h, y)

    def is_me(dev):
        return (dev[0] == x) & (dev[1] == w) & (dev[2] == c)

    from_me = x * 4 + w

    def piece(p):
        return remote(st.at[p], cg.at[from_me], S.co + p, S.co + from_me, piece_dev(p))

    def send_piece(p):
        here = is_me(piece_dev(p))

        @pl.when(here)
        def _():
            pltpu.make_async_copy(st.at[p], cg.at[from_me], recv.at[S.co + from_me]).start()

        @pl.when(jnp.logical_not(here))
        def _():
            piece(p).start()

    pl.loop(0, 5)(send_piece)

    arrive(cols_c)
    arrive(gy_all)
    for i in range(4):
        gp[i] = mm_t(gy[i].reshape(1024, 128), gc[...].reshape(1024, 512))
    gx[...] = gp[...].astype(BF16)
    for n in parts:
        for d in (2, 1, 3):
            arrived(sx.at[n, around(x, 4 - d)], S.sl + 4 * n + d)
    gz = start([remote(gx.at[around(x, d)], gr.at[x], S.gz + d, S.gz + d, at_x(around(x, d))) for d in (2, 1, 3)])

    odd = lax.rem(x, 2)

    @pl.when(c == x // 2)
    def _():
        rx[...] = sx[pl.ds(odd, 2)]

    @pl.when(c != x // 2)
    def _():
        for r in (0, 1):
            for i in range(4):
                arrived(rx.at[r, i], S.sr + 4 * r + i)

    lhs = jnp.concatenate([rx[r].reshape(768, 128) for r in (0, 1)], axis=1)
    g2[...] = mm_t(lhs, jnp.concatenate([sx[n].reshape(768, 128) for n in parts], axis=1))
    gram = g2[pl.ds(pl.multiple_of(odd * 64, 64), 192), :]
    for p in range(8):
        for n in parts:
            e2b[3 * p + n] = gram[24 * p : 24 * p + 24, 128 * n : 128 * n + 128].astype(BF16)

    def exp_dev(i, core, e):
        return (x, i, core, e // 4, lax.rem(e, 4))

    from_here = w * 8 + me

    def sum_piece(p):
        i, core, e = p // 6, lax.rem(p // 3, 2), 3 * c + lax.rem(p, 3)
        return (i == w) & (core == c) & (e == me), remote(
            e2b.at[p], er2.at[from_here], S.e2 + p, S.e2 + from_here, exp_dev(i, core, e)
        )

    @pl.loop(0, 24)
    def _(p):
        here, copy = sum_piece(p)

        @pl.when(here)
        def _():
            pltpu.make_async_copy(e2b.at[p], er2.at[from_here], recv.at[S.e2 + from_here]).start()

        @pl.when(jnp.logical_not(here))
        def _():
            copy.start()

    pl.loop(5, 16)(send_piece)

    e3 = [remote(q4, er3.at[me], S.e3 + d, S.e3 + me, exp_dev(w, c, lax.rem(me + d, 8))) for d in range(1, 8)]

    @pl.when(me < 6)
    def _():
        row = None
        for i in range(32):
            arrived(er2.at[i], S.e2 + i)
        for i in range(32):
            part = er2[i].astype(F32)
            row = part if i == 0 else row + part
        q4[...] = row * (1.0 / (EXPERTS * H))
        pltpu.make_async_copy(q4, er3.at[me], recv.at[S.e3 + me]).start()
        for copy in e3:
            copy.start()

    for i in range(16):
        pltpu.make_async_copy(cg.at[i], cg.at[i], recv.at[S.co + i]).wait()
    for i in range(4):
        for pair in (0, 1):
            even, odd = cg[4 * i + 2 * pair], cg[4 * i + 2 * pair + 1]
            at = (i % 2) * 768 + pair * 384
            coef_out[i // 2, :, at : at + 128] = even[:, 0:128]
            coef_out[i // 2, :, at + 128 : at + 256] = even[:, 128:256] + odd[:, 0:128]
            coef_out[i // 2, :, at + 256 : at + 384] = odd[:, 128:256]

    routed = gp[x]
    for copy, d in zip(gz, (2, 1, 3)):
        copy.wait_recv()
        routed += gr[around(x, 4 - d)].astype(F32)
    routed_out[...] = routed * (NROUTE / (TOP * TOKENS))

    for i in range(6):
        arrived(er3.at[i], S.e3 + i)
        gram_out[:, 128 * i : 128 * i + 128] = er3[i]

    for copy in sent:
        copy.wait_send()

    @pl.loop(0, 16)
    def _(p):
        @pl.when(jnp.logical_not(is_me(piece_dev(p))))
        def _():
            piece(p).wait_send()


    @pl.loop(0, 24)
    def _(p):
        here, copy = sum_piece(p)

        @pl.when(jnp.logical_not(here))
        def _():
            copy.wait_send()

    @pl.when(me < 6)
    def _():
        for copy in e3:
            copy.wait_send()


def whole(tokens, route_ids, whiten, deltas, basis):
    in_hbm = pl.BlockSpec(memory_space=pltpu.HBM)
    vmem = pl.BlockSpec(memory_space=pltpu.VMEM)
    return pl.pallas_call(
        kernel,
        out_shape=(
            jax.ShapeDtypeStruct((128, 512), F32),
            jax.ShapeDtypeStruct((2, 24, H), F32),
            jax.ShapeDtypeStruct((24, 768), F32),
        ),
        in_specs=[in_hbm] * 5,
        out_specs=(vmem, vmem, vmem),
        scratch_shapes=[
            pltpu.VMEM((768, 1536), BF16),
            pltpu.VMEM((8, 768), jnp.int32),
            pltpu.VMEM((4, 2, 128, 128), BF16),
            pltpu.VMEM((128, 512), BF16),
            pltpu.VMEM((4, 8, 128, 128), BF16),
            pltpu.VMEM((8, 128, 512), BF16),
            pltpu.VMEM((4, 128, 512), F32),
            pltpu.VMEM((4, 128, 512), BF16),
            pltpu.VMEM((4, 128, 512), BF16),
            pltpu.VMEM((PARTS, 8, 512, 128), BF16),
            pltpu.VMEM((PARTS, 4, 3, 128, 128), BF16),
            pltpu.VMEM((512, 4096), BF16),
            pltpu.VMEM((4, 2, 128, 768), BF16),
            pltpu.VMEM((768, 1024), BF16),
            pltpu.VMEM((PARTS, 4, 256, 128), BF16),
            pltpu.VMEM((PARTS, 512, 128), BF16),
            pltpu.VMEM((PARTS, 512, 128), F32),
            pltpu.VMEM((PARTS, 768, 128), F32),
            pltpu.VMEM((PARTS, 4, 192, 128), BF16),
            pltpu.VMEM((PARTS, 4, 192, 128), BF16),
            pltpu.VMEM((256, 384), F32),
            pltpu.VMEM((PARTS, 4, 192, 128), BF16),
            pltpu.VMEM((2, 4, 192, 128), BF16),
            pltpu.VMEM((256, 384), F32),
            pltpu.VMEM((16, 24, 256), F32),
            pltpu.VMEM((16, 24, 256), F32),
            pltpu.VMEM((24, 24, 128), BF16),
            pltpu.VMEM((32, 24, 128), BF16),
            pltpu.VMEM((24, 128), F32),
            pltpu.VMEM((6, 24, 128), F32),
            pltpu.SemaphoreType.DMA((S.total,)),
            pltpu.SemaphoreType.DMA((S.total,)),
        ],
        compiler_params=pltpu.CompilerParams(collective_id=0, has_side_effects=True, vmem_limit_bytes=52 << 20),
        cost_estimate=pl.CostEstimate(flops=4 * 10**9, bytes_accessed=20 * 10**6, transcendentals=0),
    )(*(pltpu.with_memory_space_constraint(a, pltpu.HBM) for a in (tokens, route_ids, whiten, deltas, basis)))


def shards(tokens, route_ids, whiten, deltas, basis):
    gram, coefficients, basis_gram = whole(tokens, route_ids.T, whiten, deltas, basis)
    return gram[:, None, :], coefficients.transpose(1, 0, 2), basis_gram


def solution(mesh):
    torus = Mesh(mesh.devices.reshape(4, 4, 2, 2, 4), TOK + EXP)
    placed = (P(TOK, None), P(TOK, None), P(EXP, TOK, None), P(EXP, TOK, None), P(EXP, None))
    return jax.shard_map(
        shards,
        mesh=torus,
        in_specs=placed,
        out_specs=(P(TOK, None, EXP), P(TOK, EXP, None), P(TOK, None)),
        check_vma=False,
    )
```

```python
import jax
import jax.numpy as jnp
from jax import lax
from jax.experimental import pallas as pl
from jax.experimental.pallas import tpu as pltpu
from jax.sharding import Mesh
from jax.sharding import PartitionSpec as P

H = 1536
NROUTE = 128
TOP = 8
TOKENS = 24576
EXPERTS = 16
TOK = ("x", "w", "c")
EXP = ("h", "y")
MESH = pl.DeviceIdType.MESH
F32 = jnp.float32
BF16 = jnp.bfloat16


class Ids:
    def __init__(self, **counts):
        self.total = 0
        for name, count in counts.items():
            setattr(self, name, self.total)
            self.total += count


S = Ids(
    loc=16, zq=3, fx=12, yf=12, yo=12, xo=12, wh=2, dx=4, dc=4, wx=12, tz=12, sl=12, sr=8, co=16,
    e2=32, e3=8, gd=8, gc=4, gr=4, gy=4, gz=4,
)
PARTS = 3


def mm(a, b):
    return lax.dot_general(a, b, (((1,), (0,)), ((), ())), preferred_element_type=F32)


def mm_t(a, b):
    return lax.dot_general(a, b, (((0,), (0,)), ((), ())), preferred_element_type=F32)


def kernel(
    tokens, route_ids, whiten, deltas, basis, routed_out, coef_out, gram_out,
    tk, ids, pd, pc, gy, gc, gp, gx, gr,
    bb, xq, ww, dg, dt, wg, ws, acc, tsum, ts, rz, spad, sx, rx, g2, st, cg, e2b, er2, q4, er3, send, recv,
):
    x, w, c = lax.axis_index("x"), lax.axis_index("w"), lax.axis_index("c")
    h, y = lax.axis_index("h"), lax.axis_index("y")
    me, far = h * 4 + y, (1 - h) * 4 + y
    parts = range(PARTS)
    sent = []

    def around(i, d):
        return lax.rem(i + d, 4)

    def remote(src, dst, s, r, dev):
        return pltpu.make_async_remote_copy(
            src_ref=src, dst_ref=dst, send_sem=send.at[s], recv_sem=recv.at[r], device_id=dev, device_id_type=MESH
        )

    def start(copies):
        for copy in copies:
            copy.start()
        sent.extend(copies)
        return copies

    def arrive(copies):
        for copy in copies:
            copy.wait_recv()

    def local(src, dst, n):
        copy = pltpu.make_async_copy(src, dst, recv.at[S.loc + n])
        copy.start()
        return copy

    def at_x(i):
        return (i, w, c, h, y)

    def at_w(i):
        return (x, i, c, h, y)

    def at_y(i):
        return (x, w, c, h, i)

    other = (x, w, 1 - c, h, y)
    opposite = (x, 3 - w, c, 1 - h, y)

    def columns(at, size):
        return pl.ds(pl.multiple_of(at, 128), size)

    mine = pl.multiple_of(c * 128, 128)
    basis_in = [local(basis.at[:, columns(c * 384 + 128 * n, 128)], bb.at[n, me], n) for n in parts]
    whiten_in = [local(whiten.at[e], ww.at[pl.ds(e * 256 + mine, 128)], 3 + e) for e in (0, 1)]
    ids_in = local(route_ids, ids, 5)

    def delta_part(i):
        return deltas.at[i // 2, :, columns(lax.rem(i, 2) * 768, 768)]

    delta_in = local(delta_part(x), dg.at[x, c], 6)
    token_in = [
        local(tokens.at[:, columns(1024 * y, 1024)], tk.at[:, 0:1024], 7),
        local(tokens.at[:, columns(512 * me, 512)], tk.at[:, 1024:1536], 8),
    ]

    barrier = pltpu.get_barrier_semaphore()
    friends = [(around(x, d), w, lax.rem(c + k, 2), h, y) for d in range(4) for k in (0, 1) if d or k]
    friends += [at_y(around(y, d)) for d in (1, 2, 3)] + [at_w(around(w, d)) for d in (1, 2, 3)] + [opposite]
    for dev in friends:
        pl.semaphore_signal(barrier, inc=1, device_id=dev, device_id_type=MESH)

    pl.semaphore_wait(barrier, len(friends))

    quarter = pl.ds(pl.multiple_of(x * 128, 128), 128)
    zq = [remote(bb.at[n, me, quarter], bb.at[n, me, quarter], S.zq + n, S.zq + n, opposite) for n in parts]
    fx = [
        [remote(bb.at[n, far, quarter], bb.at[n, far, quarter], S.fx + 4 * n + d, S.fx + 4 * n + d, at_x(around(x, d))) for d in (2, 1, 3)]
        for n in parts
    ]
    yf = [
        [remote(bb.at[n, far], bb.at[n, far], S.yf + 4 * n + d, S.yf + 4 * n + d, at_y(around(y, d))) for d in (1, 3, 2)]
        for n in parts
    ]
    own_y = [
        [
            remote(
                bb.at[n, me] if n == 0 else bb.at[n, me, quarter],
                bb.at[n, me] if n == 0 else xq.at[n, x, d - 1],
                S.yo + 4 * n + d, S.yo + 4 * n + d, at_y(around(y, d)),
            )
            for d in (1, 2, 3)
        ]
        for n in parts
    ]
    own_x = [
        [remote(xq.at[n, x], xq.at[n, x], S.xo + 4 * n + d, S.xo + 4 * n + d, at_x(around(x, d))) for d in (2, 1, 3)]
        for n in parts
    ]
    for n in parts:
        basis_in[n].wait()
        start([zq[n]])
    for n in parts:
        start(own_y[n])
    wh = start([remote(whiten.at[e], ww.at[pl.ds(e * 256 + mine, 128)], S.wh + e, S.wh + e, other) for e in (0, 1)])
    dc = start([remote(delta_part(x), dg.at[x, c], S.dc, S.dc, other)])

    ids_in.wait()
    hit = jnp.max(jnp.where(ids[...] == 0, 1.0, 0.0), axis=0, keepdims=True)
    hits = jnp.broadcast_to(hit, (8, 768)).astype(BF16)
    earlier = lax.broadcasted_iota(jnp.int32, (768, 768), 0) <= lax.broadcasted_iota(jnp.int32, (768, 768), 1)
    place = mm(hits, jnp.where(earlier, 1.0, 0.0).astype(BF16))[0:1]
    place = jnp.broadcast_to(jnp.where(hit > 0.0, place, 0.0), (128, 768))
    slot = (lax.broadcasted_iota(jnp.int32, (128, 768), 0) + 1).astype(F32)
    pick = jnp.where(place == slot, 1.0, 0.0).astype(BF16)

    def arrived(dst, sem):
        pltpu.make_async_copy(dst, dst, recv.at[sem]).wait()

    def factor(at, size):
        return ww[:, columns(at, size)]

    for n in parts:
        arrived(bb.at[n, far, quarter], S.zq + n)
        start(fx[n])
    dx = start([remote(delta_part(around(x, d)), dg.at[x, c], S.dx + d, S.dx + d, at_x(around(x, d))) for d in (2, 1, 3)])
    for copy in token_in:
        copy.wait()
    mine8 = 2 * w + c
    for n in range(4):
        part = mm(pick, tk[:, 256 * n : 256 * n + 256]).astype(BF16)
        pd[n, 0] = part[:, 0:128]
        pd[n, 1] = part[:, 128:256]
    pc[...] = mm(pick, tk[:, 1024:1536]).astype(BF16)
    gy[y, mine8] = pd[w, c]
    gc[mine8] = pc[...]

    for copy in whiten_in:
        copy.wait()
    arrive(wh)
    acc[0] = mm(factor(me * 512, 512), bb[0, me])
    for n in parts:
        for d in (2, 1, 3):
            arrived(bb.at[n, far, quarter], S.fx + 4 * n + d)
        start(yf[n])
        if n == 1:
            arrive(own_y[n])
            start(own_x[n])
    for n in (1, 2):
        acc[n] = mm(factor(me * 512, 512), bb[n, me])

    rows8 = start(
        [
            remote(
                pd.at[around(w, d), lax.rem(c + k, 2)], gy.at[y, mine8], S.gd + 2 * d + k, S.gd + 2 * d + k,
                (x, around(w, d), lax.rem(c + k, 2), h, y),
            )
            for d in range(4) for k in (0, 1) if d or k
        ]
    )
    cols = start([remote(pc, gc.at[mine8], S.gc + d, S.gc + d, at_w(around(w, d))) for d in (1, 2, 3)])
    cols_c = start([remote(pc, gc.at[mine8], S.gr, S.gr, other)])

    for n in parts:
        acc[n] += mm(factor(far * 512, 512), bb[n, far])

    for d in (1, 2, 3):
        block = h * 4 + around(y, 4 - d)
        arrived(bb.at[0, block], S.yo + d)
        acc[0] += mm(factor(block * 512, 512), bb[0, block])

    delta_in.wait()
    for copy, d in zip(dx, (2, 1, 3)):
        copy.wait_recv()
        src = around(x, 4 - d)
        dc += start([remote(dg.at[src, c], dg.at[src, c], S.dc + d, S.dc + d, other)])

    def from_y(d):
        return (1 - h) * 4 + around(y, 4 - d)

    def expert_rows(i):
        return pl.ds(pl.multiple_of((i // 2) * 256, 256), 256)

    def whitened(n):
        total = acc[n]
        if n:
            arrive(own_x[n])
            for d in (1, 2, 3):
                block = jnp.concatenate([xq[n, i, d - 1] for i in range(4)], axis=0)
                total += mm(factor((h * 4 + around(y, 4 - d)) * 512, 512), block)
        for d in (2, 1, 3):
            arrived(bb.at[n, from_y(d)], S.yf + 4 * n + d)
            total += mm(factor(from_y(d) * 512, 512), bb[n, from_y(d)])
        ws[n] = total.astype(BF16)
        wg[n, x] = ws[n, expert_rows(x)]
        return start(
            [
                remote(ws.at[n, expert_rows(around(x, d))], wg.at[n, x], S.wx + 4 * n + d, S.wx + 4 * n + d, at_x(around(x, d)))
                for d in (2, 1, 3)
            ]
        )

    def hidden(n, wx):
        arrive(wx)
        tsum[n] = mm(dt[...], wg[n].reshape(1024, 128))
        ts[n] = tsum[n].astype(BF16).reshape(4, 192, 128)
        return start(
            [
                remote(ts.at[n, around(w, d)], rz.at[n, w], S.tz + 4 * n + d, S.tz + 4 * n + d, at_w(around(w, d)))
                for d in (2, 1, 3)
            ]
        )

    wx0 = whitened(0)
    arrive(own_y[2])
    start(own_x[2])
    arrive(dc)
    for i in range(4):
        dt[:, 256 * i : 256 * i + 256] = dg[i].reshape(256, 768).T
    wx1 = whitened(1)
    tz = [hidden(0, wx0)]
    wx2 = whitened(2)
    arrive(rows8)
    gy_all = start([remote(gy.at[y], gy.at[y], S.gy + d, S.gy + d, at_y(around(y, d))) for d in (1, 2, 3)])
    for d in (1, 2, 3):
        cols[d - 1].wait_recv()
        src = 2 * around(w, 4 - d) + c
        cols_c += start([remote(gc.at[src], gc.at[src], S.gr + d, S.gr + d, other)])

    tz.append(hidden(1, wx1))
    tz.append(hidden(2, wx2))

    spad[...] = jnp.zeros_like(spad)
    swap, rows = [], {}
    for n in parts:
        total = tsum[n, pl.ds(pl.multiple_of(w * 192, 64), 192), :]
        for copy, d in zip(tz[n], (2, 1, 3)):
            copy.wait_recv()
            total += rz[n, around(w, 4 - d)].astype(F32)
        sx[n, x] = total.astype(BF16)
        swap.append(
            start([remote(sx.at[n, x], sx.at[n, x], S.sl + 4 * n + d, S.sl + 4 * n + d, at_x(around(x, d))) for d in (2, 1, 3)])
        )
        for j in (0, 1):
            if 0 <= n - j <= 1:
                start([remote(sx.at[n, x], rx.at[n - j, x], S.sr + 2 * n + j, S.sr + 4 * (n - j) + x, (2 * c + j, w, 1 - c, h, y))])
        spad[pl.ds(pl.multiple_of(lax.rem(w, 2) * 64, 64), 192), 128 * n : 128 * n + 128] = total
    st[...] = spad[...].T.reshape(16, 24, 256)

    def piece_dev(p):
        return (2 * c + p // 8, lax.rem(p, 8) // 2, lax.rem(p, 2), h, y)

    def is_me(dev):
        return (dev[0] == x) & (dev[1] == w) & (dev[2] == c)

    from_me = x * 4 + w

    def piece(p):
        return remote(st.at[p], cg.at[from_me], S.co + p, S.co + from_me, piece_dev(p))

    def send_piece(p):
        here = is_me(piece_dev(p))

        @pl.when(here)
        def _():
            pltpu.make_async_copy(st.at[p], cg.at[from_me], recv.at[S.co + from_me]).start()

        @pl.when(jnp.logical_not(here))
        def _():
            piece(p).start()

    pl.loop(0, 5)(send_piece)

    arrive(cols_c)
    arrive(gy_all)
    for i in range(4):
        gp[i] = mm_t(gy[i].reshape(1024, 128), gc[...].reshape(1024, 512))
    gx[...] = gp[...].astype(BF16)
    for n in parts:
        for d in (2, 1, 3):
            arrived(sx.at[n, around(x, 4 - d)], S.sl + 4 * n + d)
    gz = start([remote(gx.at[around(x, d)], gr.at[x], S.gz + d, S.gz + d, at_x(around(x, d))) for d in (2, 1, 3)])

    odd = lax.rem(x, 2)

    @pl.when(c == x // 2)
    def _():
        rx[...] = sx[pl.ds(odd, 2)]

    @pl.when(c != x // 2)
    def _():
        for r in (0, 1):
            for i in range(4):
                arrived(rx.at[r, i], S.sr + 4 * r + i)

    lhs = jnp.concatenate([rx[r].reshape(768, 128) for r in (0, 1)], axis=1)
    g2[...] = mm_t(lhs, jnp.concatenate([sx[n].reshape(768, 128) for n in parts], axis=1))
    gram = g2[pl.ds(pl.multiple_of(odd * 64, 64), 192), :]
    for p in range(8):
        for n in parts:
            e2b[3 * p + n] = gram[24 * p : 24 * p + 24, 128 * n : 128 * n + 128].astype(BF16)

    def exp_dev(i, core, e):
        return (x, i, core, e // 4, lax.rem(e, 4))

    from_here = w * 8 + me

    def sum_piece(p):
        i, core, e = p // 6, lax.rem(p // 3, 2), 3 * c + lax.rem(p, 3)
        return (i == w) & (core == c) & (e == me), remote(
            e2b.at[p], er2.at[from_here], S.e2 + p, S.e2 + from_here, exp_dev(i, core, e)
        )

    @pl.loop(0, 24)
    def _(p):
        here, copy = sum_piece(p)

        @pl.when(here)
        def _():
            pltpu.make_async_copy(e2b.at[p], er2.at[from_here], recv.at[S.e2 + from_here]).start()

        @pl.when(jnp.logical_not(here))
        def _():
            copy.start()

    pl.loop(5, 16)(send_piece)

    e3 = [remote(q4, er3.at[me], S.e3 + d, S.e3 + me, exp_dev(w, c, lax.rem(me + d, 8))) for d in range(1, 8)]

    @pl.when(me < 6)
    def _():
        row = None
        for i in range(32):
            arrived(er2.at[i], S.e2 + i)
        for i in range(32):
            part = er2[i].astype(F32)
            row = part if i == 0 else row + part
        q4[...] = row * (1.0 / (EXPERTS * H))
        pltpu.make_async_copy(q4, er3.at[me], recv.at[S.e3 + me]).start()
        for copy in e3:
            copy.start()

    for i in range(16):
        pltpu.make_async_copy(cg.at[i], cg.at[i], recv.at[S.co + i]).wait()
    for i in range(4):
        for pair in (0, 1):
            even, odd = cg[4 * i + 2 * pair], cg[4 * i + 2 * pair + 1]
            at = (i % 2) * 768 + pair * 384
            coef_out[i // 2, :, at : at + 128] = even[:, 0:128]
            coef_out[i // 2, :, at + 128 : at + 256] = even[:, 128:256] + odd[:, 0:128]
            coef_out[i // 2, :, at + 256 : at + 384] = odd[:, 128:256]

    routed = gp[x]
    for copy, d in zip(gz, (2, 1, 3)):
        copy.wait_recv()
        routed += gr[around(x, 4 - d)].astype(F32)
    routed_out[...] = routed * (NROUTE / (TOP * TOKENS))

    for i in range(6):
        arrived(er3.at[i], S.e3 + i)
        gram_out[:, 128 * i : 128 * i + 128] = er3[i]

    for copy in sent:
        copy.wait_send()

    @pl.loop(0, 16)
    def _(p):
        @pl.when(jnp.logical_not(is_me(piece_dev(p))))
        def _():
            piece(p).wait_send()


    @pl.loop(0, 24)
    def _(p):
        here, copy = sum_piece(p)

        @pl.when(jnp.logical_not(here))
        def _():
            copy.wait_send()

    @pl.when(me < 6)
    def _():
        for copy in e3:
            copy.wait_send()


def whole(tokens, route_ids, whiten, deltas, basis):
    in_hbm = pl.BlockSpec(memory_space=pltpu.HBM)
    vmem = pl.BlockSpec(memory_space=pltpu.VMEM)
    return pl.pallas_call(
        kernel,
        out_shape=(
            jax.ShapeDtypeStruct((128, 512), F32),
            jax.ShapeDtypeStruct((2, 24, H), F32),
            jax.ShapeDtypeStruct((24, 768), F32),
        ),
        in_specs=[in_hbm] * 5,
        out_specs=(vmem, vmem, vmem),
        scratch_shapes=[
            pltpu.VMEM((768, 1536), BF16),
            pltpu.VMEM((8, 768), jnp.int32),
            pltpu.VMEM((4, 2, 128, 128), BF16),
            pltpu.VMEM((128, 512), BF16),
            pltpu.VMEM((4, 8, 128, 128), BF16),
            pltpu.VMEM((8, 128, 512), BF16),
            pltpu.VMEM((4, 128, 512), F32),
            pltpu.VMEM((4, 128, 512), BF16),
            pltpu.VMEM((4, 128, 512), BF16),
            pltpu.VMEM((PARTS, 8, 512, 128), BF16),
            pltpu.VMEM((PARTS, 4, 3, 128, 128), BF16),
            pltpu.VMEM((512, 4096), BF16),
            pltpu.VMEM((4, 2, 128, 768), BF16),
            pltpu.VMEM((768, 1024), BF16),
            pltpu.VMEM((PARTS, 4, 256, 128), BF16),
            pltpu.VMEM((PARTS, 512, 128), BF16),
            pltpu.VMEM((PARTS, 512, 128), F32),
            pltpu.VMEM((PARTS, 768, 128), F32),
            pltpu.VMEM((PARTS, 4, 192, 128), BF16),
            pltpu.VMEM((PARTS, 4, 192, 128), BF16),
            pltpu.VMEM((256, 384), F32),
            pltpu.VMEM((PARTS, 4, 192, 128), BF16),
            pltpu.VMEM((2, 4, 192, 128), BF16),
            pltpu.VMEM((256, 384), F32),
            pltpu.VMEM((16, 24, 256), F32),
            pltpu.VMEM((16, 24, 256), F32),
            pltpu.VMEM((24, 24, 128), BF16),
            pltpu.VMEM((32, 24, 128), BF16),
            pltpu.VMEM((24, 128), F32),
            pltpu.VMEM((6, 24, 128), F32),
            pltpu.SemaphoreType.DMA((S.total,)),
            pltpu.SemaphoreType.DMA((S.total,)),
        ],
        compiler_params=pltpu.CompilerParams(collective_id=0, has_side_effects=True, vmem_limit_bytes=52 << 20),
        cost_estimate=pl.CostEstimate(flops=4 * 10**9, bytes_accessed=20 * 10**6, transcendentals=0),
    )(*(pltpu.with_memory_space_constraint(a, pltpu.HBM) for a in (tokens, route_ids, whiten, deltas, basis)))


def shards(tokens, route_ids, whiten, deltas, basis):
    gram, coefficients, basis_gram = whole(tokens, route_ids.T, whiten, deltas, basis)
    return gram[:, None, :], coefficients.transpose(1, 0, 2), basis_gram


def solution(mesh):
    torus = Mesh(mesh.devices.reshape(4, 4, 2, 2, 4), TOK + EXP)
    placed = (P(TOK, None), P(TOK, None), P(EXP, TOK, None), P(EXP, TOK, None), P(EXP, None))
    return jax.shard_map(
        shards,
        mesh=torus,
        in_specs=placed,
        out_specs=(P(TOK, None, EXP), P(TOK, EXP, None), P(TOK, None)),
        check_vma=False,
    )
```
